256 devices in a mesh: wide: 128 (over y, z, x), cols: 2 (over core).
Axes of the slice: x: 4, y: 4, z: 8, core: 2. Of those that a mesh axis runs over, the one named last changes fastest.
Arguments:
- factor: float32 [262144, 256], P('wide', 'cols')
- gates: float32 [8, 128, 128], replicated, may hold values from -0.5 to 0.5
- gate_layout: int32 [2048], P('wide'), may hold values from 0 to 7
- jump_masks: int32 [3], replicated, may hold values from 1 to 127
- jump_rates: float32 [3], replicated, may hold values from 0.1 to 0.4
- sketch_perm: int32 [1024], replicated, may hold values from 0 to 1023, each once
- bases: float32 [8, 64, 64], replicated, may hold values from -0.75 to 0.75
- basis_index: int32 [128, 32], P('wide'), may hold values from 0 to 7
Outputs:
- new_factor: float32 [262144, 256], P('wide', 'cols')
- weights: float32 [128, 2048], P('wide', 'cols')
The draws below stay inside these ranges and needn't reach their ends.
Inputs may be any that keep to these rules, and one draw needn't show every extreme that they name: `jump_masks`: nonzero bit masks over the high qubits. `sketch_perm`: each value appears once.
All inputs are finite; a program needn't handle non-finite values.
Results may differ from the reference program's by a relative error of at most 0.0003.
Values sent between devices are 32-bit elements; how exact they have to be, the bound alone decides.
No kernel may reach another device: no remote copies, remote signals or barrier semaphores. Data moves between devices by JAX's collectives and lax.ppermute only.
A program may use at most 64 MiB of HBM per device.

```python
import math
import jax
import jax.numpy as jnp
from jax import lax

ROWS_DEV = 2048
GATE_ORD = 128
ROT_ORD = 64
GATES = 8
BASES = 8
JUMPS = 3
NS_ITERS = 7
ROWS = 262144
RANK = 256
STACK = 1024
N_WIDE = 128


def draw_factor(key, part):
    first, second, third = jax.random.split(jax.random.fold_in(key, 11), 3)
    rough = jnp.exp(jax.random.uniform(second, (ROWS, 1), jnp.float32) * jnp.log(10.0))
    colscale = jnp.exp(jax.random.uniform(third, (1, RANK), jnp.float32) * jnp.log(4.0))
    position = jnp.arange(ROWS, dtype=jnp.float32)[:, None] / ROWS
    base = jax.random.normal(first, (ROWS, RANK), jnp.float32)
    trend = jnp.exp(jnp.log(3.0) * position)
    return (base * rough * trend * colscale / 8.0).astype(jnp.float32)


def set_ends(result, own_key, least, largest):
    shape = result.shape
    place = [jax.random.randint(jax.random.fold_in(own_key, axis), (), 0, shape[axis]) for axis in range(len(shape))]
    result = result.at[tuple(place)].set(least)
    longest = shape.index(max(shape))
    place[longest] = (place[longest] + 1) % shape[longest]
    return result.at[tuple(place)].set(largest)


def scatter_about(stream_key, dims, deviation, bound, kind=jnp.bfloat16):
    return jnp.clip(deviation * jax.random.normal(stream_key, dims, jnp.float32), -bound, bound).astype(kind)


def setup_inputs(seed: int = 0) -> dict:
    seeds = jax.random.split(jax.random.key(seed), 9)
    return {
        "factor": draw_factor(jax.random.fold_in(seeds[8], 71), 0),
        "gates": scatter_about(seeds[1], (GATES, GATE_ORD, GATE_ORD), GATE_ORD ** -0.5, 0.5, jnp.float32),
        "gate_layout": set_ends(jax.random.randint(seeds[2], (ROWS // GATE_ORD,), 0, GATES), jax.random.fold_in(seeds[2], 1), 0, GATES - 1).astype(jnp.int32),
        "jump_masks": jax.random.randint(seeds[3], (JUMPS,), 1, N_WIDE).astype(jnp.int32),
        "jump_rates": jnp.clip(jnp.exp(jax.random.uniform(seeds[4], (JUMPS,), jnp.float32, math.log(0.1), math.log(0.4))), 0.1, 0.4),
        "sketch_perm": jax.random.permutation(seeds[5], STACK).astype(jnp.int32),
        "bases": scatter_about(seeds[6], (BASES, ROT_ORD, ROT_ORD), ROT_ORD ** -0.5, 0.75, jnp.float32),
        "basis_index": set_ends(jax.random.randint(seeds[7], (N_WIDE, ROWS_DEV // ROT_ORD), 0, BASES), jax.random.fold_in(seeds[7], 1), 0, BASES - 1).astype(jnp.int32),
    }


HIGH = lax.Precision.HIGHEST

def apply_blocks(mats, index, data):
    chosen = jnp.take(mats, index, axis=0)
    return jnp.einsum('bij,bjc->bic', chosen, data, precision=HIGH)

def flip_rows(data, mask, count):
    shaped = data.reshape(count, data.shape[0] // count, data.shape[1])
    source = jnp.bitwise_xor(jnp.arange(count, dtype=jnp.int32), mask)
    return jnp.take(shaped, source, axis=0).reshape(data.shape)

def sketch_table(sketch_perm, rank):
    target = sketch_perm % rank
    sign = 1.0 - 2.0 * (sketch_perm // rank % 2).astype(jnp.float32)
    hit = target[:, None] == jnp.arange(rank, dtype=jnp.int32)[None, :]
    return jnp.where(hit, sign[:, None], jnp.zeros((), jnp.float32))

def mixed_stack(source, table, coefs, masks, count):
    rank = table.shape[1]
    total = jnp.zeros((source.shape[0], rank), jnp.float32)
    for k in range(len(coefs)):
        block = table[k * rank:(k + 1) * rank]
        term = coefs[k] * jnp.dot(source, block, precision=HIGH, preferred_element_type=jnp.float32)
        if k > 0:
            term = flip_rows(term, masks[k - 1], count)
        total = total + term
    return total

def project_block(sketch_block, moved_block, coefs, masks, count):
    parts = []
    for k in range(len(coefs)):
        left = sketch_block if k == 0 else flip_rows(sketch_block, masks[k - 1], count)
        parts.append(coefs[k] * lax.dot_general(left, moved_block, (((0,), (0,)), ((), ())), precision=HIGH, preferred_element_type=jnp.float32))
    return jnp.concatenate(parts, axis=1)

def newton_root(mat, eye):
    fro = jnp.sqrt(jnp.sum(mat * mat))
    approx = mat / (fro + 1e-06)
    inverse = eye
    for step in range(NS_ITERS):
        middle = 1.5 * eye - 0.5 * jnp.dot(inverse, approx, precision=HIGH)
        approx = jnp.dot(approx, middle, precision=HIGH)
        inverse = jnp.dot(middle, inverse, precision=HIGH)
    return (approx, inverse, fro)

def reference(factor, gates, gate_layout, jump_masks, jump_rates, sketch_perm, bases, basis_index):
    lows = ROWS_DEV // N_WIDE
    blocks = factor.reshape(N_WIDE, ROWS_DEV // GATE_ORD, GATE_ORD, RANK)
    layout = gate_layout.reshape(N_WIDE, ROWS_DEV // GATE_ORD)
    gated = lax.map(lambda pair: apply_blocks(gates, pair[1], pair[0]), (blocks, layout))
    moved = gated.reshape(N_WIDE, N_WIDE, lows, RANK).transpose(1, 0, 2, 3).reshape(N_WIDE, ROWS_DEV, RANK)
    keep = 1.0 - 0.5 * jnp.sum(jump_rates)
    coefs = [keep] + [jnp.sqrt(jump_rates[k]) for k in range(JUMPS)]
    table = sketch_table(sketch_perm, RANK)
    sketch = lax.map(lambda block: mixed_stack(block, table, coefs, jump_masks, N_WIDE), moved)
    partial_grams = lax.map(lambda block: lax.dot_general(block, block, (((0,), (0,)), ((), ())), precision=HIGH, preferred_element_type=jnp.float32), sketch)
    gram = lax.optimization_barrier(jnp.sum(partial_grams, axis=0))
    eye = jnp.eye(RANK, dtype=jnp.float32)
    unused, inverse, fro = newton_root(gram, eye)
    partial_proj = lax.map(lambda pair: project_block(pair[0], pair[1], coefs, jump_masks, N_WIDE), (sketch, moved))
    proj = lax.optimization_barrier(jnp.sum(partial_proj, axis=0))
    coeff = lax.dot_general(inverse, proj, (((0,), (0,)), ((), ())), precision=HIGH, preferred_element_type=jnp.float32)
    core = lax.dot_general(coeff, coeff, (((1,), (1,)), ((), ())), precision=HIGH, preferred_element_type=jnp.float32)
    approx_two, unused_two, fro_two = newton_root(core, eye)
    root = jnp.sqrt(fro_two + 1e-06) * approx_two
    mixing = jnp.dot(inverse, root, precision=HIGH)
    new_blocks = lax.map(lambda block: jnp.dot(block, mixing, precision=HIGH), sketch)
    rotated_in = new_blocks.reshape(N_WIDE, ROWS_DEV // ROT_ORD, ROT_ORD, RANK)

    def outcome(pair):
        rotated = apply_blocks(bases, pair[1], pair[0])
        return lax.optimization_barrier(jnp.sum(rotated * rotated, axis=2)).reshape(ROWS_DEV) / RANK
    weights = lax.map(outcome, (rotated_in, basis_index))
    return (new_blocks.reshape(ROWS, RANK), weights)
```

```python
import jax
import jax.numpy as jnp
from jax import lax
from jax.experimental import pallas as pl
from jax.experimental.pallas import tpu as pltpu
from jax.sharding import PartitionSpec as P

NS_ITERS = 7
F32 = jnp.float32
BF16 = jnp.bfloat16
NN = (((1,), (0,)), ((), ()))
NT = (((1,), (1,)), ((), ()))


def split(x):
    hi = x.astype(BF16)
    return hi, (x - hi.astype(F32)).astype(BF16)


def dot(a, b, dims=NN):
    return lax.dot_general(a, b, dims, preferred_element_type=F32)


def mul3(a, b, dims=NN):
    return dot(a[0], b[0], dims) + (dot(a[1], b[0], dims) + dot(a[0], b[1], dims))


def gate_kernel(order, layout, gates, factor, out):
    def block(b, carry):
        rows = pl.ds(pl.multiple_of(b * order, order), order)
        out[rows, :] = mul3(split(gates[layout[b]]), split(factor[rows, :]))
        return carry

    lax.fori_loop(0, factor.shape[0] // order, block, 0)


def apply_gates(gates, layout, factor):
    order = gates.shape[1]
    return pl.pallas_call(
        lambda *refs: gate_kernel(order, *refs),
        out_shape=jax.ShapeDtypeStruct(factor.shape, F32),
        in_specs=[
            pl.BlockSpec(memory_space=pltpu.SMEM),
            pl.BlockSpec(memory_space=pltpu.VMEM),
            pl.BlockSpec(memory_space=pltpu.VMEM),
        ],
        out_specs=pl.BlockSpec(memory_space=pltpu.VMEM),
        name="gates",
    )(layout, gates, factor)


def stack_kernel(masks, rates, moved, table, sketch, proj, high, low):
    count, halves, lows, width = moved.shape
    rank = halves * width
    jumps = masks.shape[0]
    total = rates[0]
    for k in range(1, jumps):
        total = total + rates[k]
    coefs = [jnp.full((2 * lows, width), 1.0 - 0.5 * total, F32)]
    for k in range(jumps):
        coefs.append(jnp.sqrt(jnp.full((2 * lows, width), rates[k], F32)))

    def pair(p, carry):
        rows = pl.ds(pl.multiple_of(p * 2 * lows, 2 * lows), 2 * lows)
        for k in range(jumps + 1):
            flip = 0 if k == 0 else masks[k - 1]
            first, second = (2 * p) ^ flip, (2 * p + 1) ^ flip
            for c in range(halves):
                value = coefs[k] * jnp.concatenate([moved[first, c], moved[second, c]], axis=0)
                cols = slice(k * rank + c * width, k * rank + (c + 1) * width)
                high[rows, cols], low[rows, cols] = split(value)
        return carry

    lax.fori_loop(0, count // 2, pair, 0, unroll=4)
    value = dot(high[...], table[...]) + dot(low[...], table[...])
    sketch[...] = value
    left = split(value.T)
    for k in range(jumps + 1):
        cols = slice(k * rank, (k + 1) * rank)
        proj[:, cols] = mul3(left, (high[:, cols], low[:, cols]))


def stack_products(masks, rates, moved, table):
    count, halves, lows, width = moved.shape
    rows, rank = count * lows, halves * width
    columns = table.shape[0]
    vmem = pl.BlockSpec(memory_space=pltpu.VMEM)
    smem = pl.BlockSpec(memory_space=pltpu.SMEM)
    return pl.pallas_call(
        stack_kernel,
        out_shape=(
            jax.ShapeDtypeStruct((rows, rank), F32),
            jax.ShapeDtypeStruct((rank, columns), F32),
        ),
        in_specs=[smem, smem, vmem, vmem],
        out_specs=(vmem, vmem),
        scratch_shapes=[pltpu.VMEM((rows, columns), BF16), pltpu.VMEM((rows, columns), BF16)],
        compiler_params=pltpu.CompilerParams(vmem_limit_bytes=40 << 20),
        name="stack",
    )(masks, rates, moved, table)


def rotate_kernel(where, index, sketch, bases, sk_high, sk_low, rot_high, rot_low, rotated):
    halves, count, lows, rank = sketch.shape
    order = bases.shape[1]
    group = order // (halves * lows)
    blocks = rotated.shape[0] // order
    own = where[0]

    def block(b, carry):
        first = own * (count // halves) + b * group
        parts = []
        for g in range(group):
            for c in range(halves):
                parts.append(sketch[c, first + g])
        data = jnp.concatenate(parts, axis=0)
        rows = pl.ds(pl.multiple_of(b * order, order), order)
        rotated[rows, :] = mul3(split(bases[index[0, own * blocks + b]]), split(data))
        return carry

    lax.fori_loop(0, blocks, block, 0)
    rot_high[...], rot_low[...] = split(rotated[...].T)
    for c in range(halves):
        sk_high[c], sk_low[c] = split(sketch[c].reshape(count * lows, rank))


def rotate_sketch(where, index, sketch, bases):
    halves, count, lows, rank = sketch.shape
    rows = count * lows
    vmem = pl.BlockSpec(memory_space=pltpu.VMEM)
    smem = pl.BlockSpec(memory_space=pltpu.SMEM)
    return pl.pallas_call(
        rotate_kernel,
        out_shape=(
            jax.ShapeDtypeStruct((halves, rows, rank), BF16),
            jax.ShapeDtypeStruct((halves, rows, rank), BF16),
            jax.ShapeDtypeStruct((rank, rows), BF16),
            jax.ShapeDtypeStruct((rank, rows), BF16),
        ),
        in_specs=[smem, smem, vmem, vmem],
        out_specs=(vmem, vmem, vmem, vmem),
        scratch_shapes=[pltpu.VMEM((rows, rank), F32)],
        compiler_params=pltpu.CompilerParams(vmem_limit_bytes=40 << 20),
        name="rotate",
    )(where, index, sketch, bases)


def frobenius(mat):
    return jnp.sqrt(jnp.sum(jnp.sum(mat * mat, axis=0, keepdims=True), axis=1, keepdims=True))


def eye(n):
    return (
        lax.broadcasted_iota(jnp.int32, (n, n), 0) == lax.broadcasted_iota(jnp.int32, (n, n), 1)
    ).astype(F32)


def newton(mat, value):
    t = mat
    held = None
    for step in range(NS_ITERS):
        last = step == NS_ITERS - 1
        right = split(t)
        if step == 0:
            once = 1.5 * t - 0.5 * mul3(right, right)
            held = 1.5 * eye(t.shape[0]) - 0.5 * t if value is None else once
        else:
            if not last:
                once = 1.5 * t - 0.5 * mul3(right, right)
            held = 1.5 * held - 0.5 * mul3(split(held), right)
        if not last:
            t = 1.5 * once - 0.5 * mul3(split(once), right)
    return held


def output_kernel(where, proj, table, sk_high, sk_low, rot_high, rot_low, new, weights):
    rank = proj.shape[0]
    halves = sk_high.shape[0]
    width = rank // halves
    p = split(proj[...])
    gram = dot(p[0], table[...]) + dot(p[1], table[...])
    inverse = newton(gram / (frobenius(gram) + 1e-6), None)
    inv = split(inverse)
    coeff = split(mul3(inv, p))
    core = mul3(coeff, coeff, NT)
    shift = frobenius(core) + 1e-6
    root = split(newton(core / shift, "approx"))
    scale = jnp.sqrt(shift)
    mixing = scale * mul3(inv, root)
    turned = split(scale * mul3(root, inv))
    own = jnp.where(where[0] == 0, mixing[:, :width], mixing[:, width:])
    own = split(own)
    rot = mul3(turned, (rot_high[...], rot_low[...]))
    weights[...] = jnp.sum(rot * rot, axis=0, keepdims=True) / rank
    for c in range(halves):
        value = mul3((sk_high[c], sk_low[c]), own)
        new[:, c] = value.reshape(new.shape[0], new.shape[2], width)


def outputs(where, proj, table, sk_high, sk_low, rot_high, rot_low, lows):
    halves, rows, rank = sk_high.shape
    vmem = pl.BlockSpec(memory_space=pltpu.VMEM)
    smem = pl.BlockSpec(memory_space=pltpu.SMEM)
    return pl.pallas_call(
        output_kernel,
        out_shape=(
            jax.ShapeDtypeStruct((rows // lows, halves, lows, rank // halves), F32),
            jax.ShapeDtypeStruct((1, rows), F32),
        ),
        in_specs=[smem] + [vmem] * 6,
        out_specs=(vmem, vmem),
        compiler_params=pltpu.CompilerParams(vmem_limit_bytes=40 << 20),
        name="outputs",
    )(where, proj, table, sk_high, sk_low, rot_high, rot_low)


def sketch_table(sketch_perm, rank):
    target = sketch_perm % rank
    sign = 1.0 - 2.0 * (sketch_perm // rank % 2).astype(F32)
    hit = target[:, None] == jnp.arange(rank, dtype=jnp.int32)[None, :]
    return jnp.where(hit, sign[:, None], jnp.zeros((), F32)).astype(BF16)


def per_device(factor, gates, gate_layout, jump_masks, jump_rates, sketch_perm, bases, basis_index):
    rows, width = factor.shape
    count = lax.axis_size("wide")
    halves = lax.axis_size("cols")
    rank = width * halves
    lows = rows // (count * halves)
    where = lax.axis_index("cols").astype(jnp.int32).reshape(1)
    gated = apply_gates(gates, gate_layout, factor)
    pieces = gated.reshape(count * halves, lows, width)
    moved = lax.all_to_all(pieces, ("wide", "cols"), split_axis=0, concat_axis=0, tiled=True)
    moved = moved.reshape(count, halves, lows, width)
    table = sketch_table(sketch_perm, rank)
    sketch_own, proj_own = stack_products(jump_masks, jump_rates, moved, table)
    proj = lax.psum(proj_own, ("wide", "cols"))
    sketch = lax.all_gather(sketch_own, "cols", axis=0, tiled=False)
    sketch = sketch.reshape(halves, count, lows, rank)
    sk_high, sk_low, rot_high, rot_low = rotate_sketch(where, basis_index, sketch, bases)
    new, weights = outputs(where, proj, table, sk_high, sk_low, rot_high, rot_low, lows)
    return new.reshape(rows, width), weights


def solution(mesh):
    return jax.shard_map(
        per_device,
        mesh=mesh,
        in_specs=(P("wide", "cols"), P(), P("wide"), P(), P(), P(), P(), P("wide", None)),
        out_specs=(P("wide", "cols"), P("wide", "cols")),
        check_vma=False,
    )
```

```python
import jax
import jax.numpy as jnp
from jax import lax
from jax.experimental import pallas as pl
from jax.experimental.pallas import tpu as pltpu
from jax.sharding import PartitionSpec as P

NS_ITERS = 7
F32 = jnp.float32
BF16 = jnp.bfloat16
NN = (((1,), (0,)), ((), ()))
NT = (((1,), (1,)), ((), ()))


def split(x):
    hi = x.astype(BF16)
    return hi, (x - hi.astype(F32)).astype(BF16)


def dot(a, b, dims=NN):
    return lax.dot_general(a, b, dims, preferred_element_type=F32)


def mul3(a, b, dims=NN):
    return dot(a[0], b[0], dims) + (dot(a[1], b[0], dims) + dot(a[0], b[1], dims))


def gate_kernel(order, where, layout, gates, factor, keep, send):
    lows = keep.shape[1]
    group = order // (2 * lows)
    mine = where[0] == 0
    for b in range(factor.shape[0] // order):
        high, low = split(factor[b * order : (b + 1) * order, :])
        left = jnp.concatenate(split(gates[layout[b]]), axis=1)
        right = jnp.concatenate(
            [
                jnp.concatenate([high, low], axis=1),
                jnp.concatenate([high, jnp.zeros_like(high)], axis=1),
            ],
            axis=0,
        )
        both = dot(left, right)
        value = both[:, : high.shape[1]] + both[:, high.shape[1] :]
        value = value.reshape(group, 2, lows, high.shape[1])
        hs = slice(b * group, (b + 1) * group)
        keep[hs] = jnp.where(mine, value[:, 0], value[:, 1])
        send[hs] = jnp.where(mine, value[:, 1], value[:, 0])


def apply_gates(where, gates, layout, factor, count):
    order = gates.shape[1]
    rows, width = factor.shape
    vmem = pl.BlockSpec(memory_space=pltpu.VMEM)
    smem = pl.BlockSpec(memory_space=pltpu.SMEM)
    half = jax.ShapeDtypeStruct((count, rows // (2 * count), width), F32)
    return pl.pallas_call(
        lambda *refs: gate_kernel(order, *refs),
        out_shape=(half, half),
        in_specs=[smem, smem, vmem, vmem],
        out_specs=(vmem, vmem),
        name="gates",
    )(where, layout, gates, factor)


def join_kernel(where, kept, received, out):
    width = kept.shape[2]
    first = pl.multiple_of(where[0] * width, width)
    second = pl.multiple_of((1 - where[0]) * width, width)
    out[:, :, pl.ds(first, width)] = kept[...]
    out[:, :, pl.ds(second, width)] = received[...]


def join_columns(where, kept, received):
    count, lows, width = kept.shape
    vmem = pl.BlockSpec(memory_space=pltpu.VMEM)
    return pl.pallas_call(
        join_kernel,
        out_shape=jax.ShapeDtypeStruct((count, lows, 2 * width), F32),
        in_specs=[pl.BlockSpec(memory_space=pltpu.SMEM), vmem, vmem],
        out_specs=vmem,
        name="join",
    )(where, kept, received)


def stack_kernel(where, masks, rates, moved, table, sketch, keep, send, high, low):
    count, lows, rank = moved.shape
    jumps = masks.shape[0]
    total = rates[0]
    for k in range(1, jumps):
        total = total + rates[k]
    coefs = [jnp.full((2 * lows, rank), 1.0 - 0.5 * total, F32)]
    for k in range(jumps):
        coefs.append(jnp.sqrt(jnp.full((2 * lows, rank), rates[k], F32)))

    def pair(p, carry):
        rows = pl.ds(pl.multiple_of(p * 2 * lows, 2 * lows), 2 * lows)
        for k in range(jumps + 1):
            flip = 0 if k == 0 else masks[k - 1]
            first, second = (2 * p) ^ flip, (2 * p + 1) ^ flip
            value = coefs[k] * jnp.concatenate([moved[first], moved[second]], axis=0)
            cols = slice(k * rank, (k + 1) * rank)
            high[rows, cols], low[rows, cols] = split(value)
        return carry

    lax.fori_loop(0, count // 2, pair, 0, unroll=4)
    value = dot(high[...], table[...]) + dot(low[...], table[...])
    sketch[...] = value.reshape(sketch.shape)
    left = split(value.T)
    mine = where[0] == 0
    half = rank // 2
    for k in range(jumps + 1):
        cols = slice(k * rank, (k + 1) * rank)
        part = mul3(left, (high[:, cols], low[:, cols]))
        for j in range(rank // 128):
            tiles = part[:, j * 128 : (j + 1) * 128]
            top = tiles[:half].reshape(half // 8, 8, 128)
            bottom = tiles[half:].reshape(half // 8, 8, 128)
            keep[:, k * (rank // 128) + j] = jnp.where(mine, top, bottom)
            send[:, k * (rank // 128) + j] = jnp.where(mine, bottom, top)


def stack_products(where, masks, rates, moved, table):
    count, lows, rank = moved.shape
    columns = table.shape[0]
    vmem = pl.BlockSpec(memory_space=pltpu.VMEM)
    smem = pl.BlockSpec(memory_space=pltpu.SMEM)
    half = jax.ShapeDtypeStruct((rank // 16, columns // 128, 8, 128), F32)
    return pl.pallas_call(
        stack_kernel,
        out_shape=(jax.ShapeDtypeStruct(moved.shape, F32), half, half),
        in_specs=[smem, smem, smem, vmem, vmem],
        out_specs=(vmem, vmem, vmem),
        scratch_shapes=[pltpu.VMEM((count * lows, columns), BF16)] * 2,
        compiler_params=pltpu.CompilerParams(vmem_limit_bytes=40 << 20),
        name="stack",
    )(where, masks, rates, moved, table)


def spread_kernel(parts, out):
    out[...] = jnp.broadcast_to(jnp.sum(parts[...], axis=0, keepdims=True), out.shape)


def sum_wide(part, beside):
    vmem = pl.BlockSpec(memory_space=pltpu.VMEM)
    pieces = lax.all_to_all(part, "wide", split_axis=0, concat_axis=0, tiled=True)
    pieces, beside = lax.optimization_barrier((pieces, beside))
    copies = pl.pallas_call(
        spread_kernel,
        out_shape=jax.ShapeDtypeStruct(part.shape, F32),
        in_specs=[vmem],
        out_specs=vmem,
        name="spread",
    )(pieces)
    total = lax.all_to_all(copies, "wide", split_axis=0, concat_axis=0, tiled=True)
    return total, beside


def rotate_kernel(where, index, own, other, bases, sk_high, sk_low, rot_high, rot_low, rotated):
    count, lows, rank = own.shape
    order = bases.shape[1]
    group = order // (2 * lows)
    blocks = rotated.shape[0] // order
    core = where[0]
    mine = core == 0
    for b in range(blocks):
        parts = []
        for g in range(group):
            w = core * (count // 2) + b * group + g
            first, second = own[w], other[w]
            parts.append(jnp.where(mine, first, second))
            parts.append(jnp.where(mine, second, first))
        data = jnp.concatenate(parts, axis=0)
        value = mul3(split(bases[index[0, core * blocks + b]]), split(data))
        rotated[b * order : (b + 1) * order, :] = value
    rot_high[...], rot_low[...] = split(rotated[...].T)
    sk_high[core], sk_low[core] = split(own[...].reshape(count * lows, rank))
    sk_high[1 - core], sk_low[1 - core] = split(other[...].reshape(count * lows, rank))


def rotate_sketch(where, index, own, other, bases):
    count, lows, rank = own.shape
    rows = count * lows
    vmem = pl.BlockSpec(memory_space=pltpu.VMEM)
    smem = pl.BlockSpec(memory_space=pltpu.SMEM)
    return pl.pallas_call(
        rotate_kernel,
        out_shape=(
            jax.ShapeDtypeStruct((2, rows, rank), BF16),
            jax.ShapeDtypeStruct((2, rows, rank), BF16),
            jax.ShapeDtypeStruct((rank, rows), BF16),
            jax.ShapeDtypeStruct((rank, rows), BF16),
        ),
        in_specs=[smem, smem, vmem, vmem, vmem],
        out_specs=(vmem, vmem, vmem, vmem),
        scratch_shapes=[pltpu.VMEM((rows, rank), F32)],
        compiler_params=pltpu.CompilerParams(vmem_limit_bytes=40 << 20),
        name="rotate",
    )(where, index, own, other, bases)


def frobenius(mat):
    return jnp.sqrt(jnp.sum(jnp.sum(mat * mat, axis=0, keepdims=True), axis=1, keepdims=True))


def eye(n):
    return (
        lax.broadcasted_iota(jnp.int32, (n, n), 0) == lax.broadcasted_iota(jnp.int32, (n, n), 1)
    ).astype(F32)


def newton(mat, value):
    t = mat
    held = None
    for step in range(NS_ITERS):
        last = step == NS_ITERS - 1
        right = split(t)
        if step == 0:
            once = 1.5 * t - 0.5 * mul3(right, right)
            held = 1.5 * eye(t.shape[0]) - 0.5 * t if value is None else once
        else:
            if not last:
                once = 1.5 * t - 0.5 * mul3(right, right)
            held = 1.5 * held - 0.5 * mul3(split(held), right)
        if not last:
            t = 1.5 * once - 0.5 * mul3(split(once), right)
    return held


def output_kernel(
    where, mine, other, table, sk_high, sk_low, rot_high, rot_low, new, weights, proj
):
    rank = proj.shape[0]
    halves = sk_high.shape[0]
    width = rank // halves
    first = pl.ds(pl.multiple_of(where[0] * width, width), width)
    second = pl.ds(pl.multiple_of((1 - where[0]) * width, width), width)
    for j in range(mine.shape[1]):
        cols = slice(j * 128, (j + 1) * 128)
        proj[first, cols] = mine[:, j].reshape(width, 128)
        proj[second, cols] = other[:, j].reshape(width, 128)
    p = split(proj[...])
    gram = dot(p[0], table[...]) + dot(p[1], table[...])
    inverse = newton(gram / (frobenius(gram) + 1e-6), None)
    inv = split(inverse)
    coeff = split(mul3(inv, p))
    core = mul3(coeff, coeff, NT)
    shift = frobenius(core) + 1e-6
    root = split(newton(core / shift, "approx"))
    scale = jnp.sqrt(shift)
    mixing = scale * mul3(inv, root)
    turned = split(scale * mul3(root, inv))
    own = jnp.where(where[0] == 0, mixing[:, :width], mixing[:, width:])
    own = split(own)
    rot = mul3(turned, (rot_high[...], rot_low[...]))
    weights[...] = jnp.sum(rot * rot, axis=0, keepdims=True) / rank
    for c in range(halves):
        value = mul3((sk_high[c], sk_low[c]), own)
        new[:, c] = value.reshape(new.shape[0], new.shape[2], width)


def outputs(where, mine, other, table, sk_high, sk_low, rot_high, rot_low, lows):
    halves, rows, rank = sk_high.shape
    vmem = pl.BlockSpec(memory_space=pltpu.VMEM)
    smem = pl.BlockSpec(memory_space=pltpu.SMEM)
    return pl.pallas_call(
        output_kernel,
        out_shape=(
            jax.ShapeDtypeStruct((rows // lows, halves, lows, rank // halves), F32),
            jax.ShapeDtypeStruct((1, rows), F32),
        ),
        in_specs=[smem] + [vmem] * 7,
        out_specs=(vmem, vmem),
        scratch_shapes=[pltpu.VMEM((rank, table.shape[0]), F32)],
        compiler_params=pltpu.CompilerParams(vmem_limit_bytes=40 << 20),
        name="outputs",
    )(where, mine, other, table, sk_high, sk_low, rot_high, rot_low)


def sketch_table(sketch_perm, rank):
    target = sketch_perm % rank
    sign = 1.0 - 2.0 * (sketch_perm // rank % 2).astype(F32)
    hit = target[:, None] == jnp.arange(rank, dtype=jnp.int32)[None, :]
    return jnp.where(hit, sign[:, None], jnp.zeros((), F32)).astype(BF16)


def swap(value):
    return lax.ppermute(value, "cols", [(0, 1), (1, 0)])


def per_device(factor, gates, gate_layout, jump_masks, jump_rates, sketch_perm, bases, basis_index):
    rows, width = factor.shape
    count = lax.axis_size("wide")
    rank = width * lax.axis_size("cols")
    lows = rows // (2 * count)
    where = lax.axis_index("cols").astype(jnp.int32).reshape(1)
    kept, sent = apply_gates(where, gates, gate_layout, factor, count)
    pieces = join_columns(where, kept, swap(sent))
    moved = lax.all_to_all(pieces, "wide", split_axis=0, concat_axis=0, tiled=True)
    table = sketch_table(sketch_perm, rank)
    sketch, keep, send = stack_products(where, jump_masks, jump_rates, moved, table)
    part = keep + swap(send)
    total, other = sum_wide(part.reshape(-1, 8, 128), swap(sketch))
    turned = rotate_sketch(where, basis_index, sketch, other, bases)
    total, turned = lax.optimization_barrier((total.reshape(part.shape), turned))
    new, weights = outputs(where, total, swap(total), table, *turned, lows)
    return new.reshape(rows, width), weights


def solution(mesh):
    return jax.shard_map(
        per_device,
        mesh=mesh,
        in_specs=(P("wide", "cols"), P(), P("wide"), P(), P(), P(), P(), P("wide", None)),
        out_specs=(P("wide", "cols"), P("wide", "cols")),
        check_vma=False,
    )
```

```python
import jax
import jax.numpy as jnp
from jax import lax
from jax.experimental import pallas as pl
from jax.experimental.pallas import tpu as pltpu
from jax.sharding import PartitionSpec as P

NS_ITERS = 7
F32 = jnp.float32
BF16 = jnp.bfloat16
NN = (((1,), (0,)), ((), ()))
NT = (((1,), (1,)), ((), ()))


def split(x):
    hi = x.astype(BF16)
    return hi, (x - hi.astype(F32)).astype(BF16)


def dot(a, b, dims=NN):
    return lax.dot_general(a, b, dims, preferred_element_type=F32)


def mul3(a, b, dims=NN):
    left = jnp.concatenate([a[0], a[1], a[0]], axis=dims[0][0][0])
    right = jnp.concatenate([b[0], b[0], b[1]], axis=dims[0][1][0])
    return dot(left, right, dims)


def params(mib):
    return pltpu.CompilerParams(vmem_limit_bytes=mib << 20)


def gate_kernel(order, where, layout, gates, factor, keep, send):
    lows, width = send.shape[1:]
    group = order // (2 * lows)
    blocks = factor.shape[0] // order
    mine = where[0] == 0
    for b in range(blocks):
        high, low = split(factor[b * order : (b + 1) * order, :])
        left = jnp.concatenate(split(gates[layout[pl.program_id(0) * blocks + b]]), axis=1)
        right = jnp.concatenate(
            [
                jnp.concatenate([high, low], axis=1),
                jnp.concatenate([high, jnp.zeros_like(high)], axis=1),
            ],
            axis=0,
        )
        both = dot(left, right)
        value = both[:, :width] + both[:, width:]
        value = value.reshape(group, 2, lows, width)
        hs = slice(b * group, (b + 1) * group)
        keep[hs, 0] = jnp.where(mine, value[:, 0], value[:, 1])
        send[hs] = jnp.where(mine, value[:, 1], value[:, 0])


def apply_gates(where, gates, layout, factor, count):
    order = gates.shape[1]
    rows, width = factor.shape
    lows = rows // (2 * count)
    steps = 2
    return pl.pallas_call(
        lambda *refs: gate_kernel(order, *refs),
        out_shape=(
            jax.ShapeDtypeStruct((count, 2, lows, width), F32),
            jax.ShapeDtypeStruct((count, lows, width), F32),
        ),
        grid_spec=pltpu.PrefetchScalarGridSpec(
            num_scalar_prefetch=2,
            grid=(steps,),
            in_specs=[
                pl.BlockSpec(gates.shape, lambda i, where, layout: (0, 0, 0)),
                pl.BlockSpec((rows // steps, width), lambda i, where, layout: (i, 0)),
            ],
            out_specs=(
                pl.BlockSpec(
                    (count // steps, 1, lows, width), lambda i, where, layout: (i, where[0], 0, 0)
                ),
                pl.BlockSpec((count // steps, lows, width), lambda i, where, layout: (i, 0, 0)),
            ),
        ),
        compiler_params=params(8),
        name="gates",
    )(where, layout, gates, factor)


def join_kernel(where, received, kept, joined, sem):
    copy = pltpu.make_async_copy(received, joined.at[:, 1 - where[0]], sem)
    copy.start()
    copy.wait()


def join_columns(where, received, kept):
    away = pl.BlockSpec(memory_space=pl.ANY)
    return pl.pallas_call(
        join_kernel,
        out_shape=jax.ShapeDtypeStruct(kept.shape, F32),
        in_specs=[pl.BlockSpec(memory_space=pltpu.SMEM), away, away],
        out_specs=away,
        scratch_shapes=[pltpu.SemaphoreType.DMA(())],
        input_output_aliases={2: 0},
        compiler_params=params(1),
        name="join",
    )(where, received, kept)


def stack_kernel(where, masks, rates, moved, table, sketch, keep, send, high, low):
    count, halves, lows, width = moved.shape
    rank = halves * width
    jumps = masks.shape[0]
    total = rates[0]
    for k in range(1, jumps):
        total = total + rates[k]
    coefs = [jnp.full((2 * lows, width), 1.0 - 0.5 * total, F32)]
    for k in range(jumps):
        coefs.append(jnp.sqrt(jnp.full((2 * lows, width), rates[k], F32)))

    def pair(p, carry):
        rows = pl.ds(pl.multiple_of(p * 2 * lows, 2 * lows), 2 * lows)
        for k in range(jumps + 1):
            flip = 0 if k == 0 else masks[k - 1]
            first, second = (2 * p) ^ flip, (2 * p + 1) ^ flip
            for c in range(halves):
                value = coefs[k] * jnp.concatenate([moved[first, c], moved[second, c]], axis=0)
                cols = slice(k * rank + c * width, k * rank + (c + 1) * width)
                high[rows, cols], low[rows, cols] = split(value)
        return carry

    lax.fori_loop(0, count // 2, pair, 0, unroll=4)
    value = dot(high[...], table[...]) + dot(low[...], table[...])
    sketch[...] = value.reshape(sketch.shape)
    left = split(value.T)
    mine = where[0] == 0
    half = rank // 2
    for k in range(jumps + 1):
        cols = slice(k * rank, (k + 1) * rank)
        part = mul3(left, (high[:, cols], low[:, cols]))
        for j in range(rank // 128):
            tiles = part[:, j * 128 : (j + 1) * 128]
            top = tiles[:half].reshape(half // 8, 8, 128)
            bottom = tiles[half:].reshape(half // 8, 8, 128)
            keep[:, k * (rank // 128) + j] = jnp.where(mine, top, bottom)
            send[:, k * (rank // 128) + j] = jnp.where(mine, bottom, top)


def stack_products(where, masks, rates, moved, table):
    count, halves, lows, width = moved.shape
    rank = halves * width
    columns = table.shape[0]
    vmem = pl.BlockSpec(memory_space=pltpu.VMEM)
    smem = pl.BlockSpec(memory_space=pltpu.SMEM)
    half = jax.ShapeDtypeStruct((rank // 16, columns // 128, 8, 128), F32)
    return pl.pallas_call(
        stack_kernel,
        out_shape=(jax.ShapeDtypeStruct((count, lows, rank), F32), half, half),
        in_specs=[smem, smem, smem, vmem, vmem],
        out_specs=(vmem, vmem, vmem),
        scratch_shapes=[pltpu.VMEM((count * lows, columns), BF16)] * 2,
        compiler_params=params(20),
        name="stack",
    )(where, masks, rates, moved, table)


SIDES = (4, 8, 4)


def groups(count):
    ny, nz, nx = SIDES
    assert ny * nz * nx == count
    at = lambda y, z, x: (y * nz + z) * nx + x
    planes = [[at(y, z, x) for y in range(ny) for x in range(nx)] for z in range(nz)]
    lines = [[at(y, z, x) for z in range(nz)] for y in range(ny) for x in range(nx)]
    return planes, lines


def spread_kernel(parts, out):
    out[...] = jnp.broadcast_to(jnp.sum(parts[...], axis=0, keepdims=True), out.shape)


def sum_and_spread(parts, copies):
    vmem = pl.BlockSpec(memory_space=pltpu.VMEM)
    return pl.pallas_call(
        spread_kernel,
        out_shape=jax.ShapeDtypeStruct((copies,) + parts.shape[1:], F32),
        in_specs=[vmem],
        out_specs=vmem,
        compiler_params=params(4),
        name="spread",
    )(parts)


def exchange(pieces, members):
    return lax.all_to_all(
        pieces, "wide", split_axis=0, concat_axis=0, axis_index_groups=members, tiled=True
    )


def sum_wide(part, beside):
    planes, lines = groups(lax.axis_size("wide"))
    assert len(planes[0]) == part.shape[0]
    pieces = exchange(part, planes)
    pieces, beside = lax.optimization_barrier((pieces, beside))
    pieces = exchange(sum_and_spread(pieces, len(lines[0])), lines)
    return exchange(sum_and_spread(pieces, len(planes[0])), planes), beside


def rotate_kernel(where, index, own, other, bases, sk_high, sk_low, rot_high, rot_low, rotated):
    count, lows, rank = own.shape
    order = bases.shape[1]
    group = order // (2 * lows)
    blocks = rotated.shape[0] // order
    core = where[0]
    mine = core == 0
    for b in range(blocks):
        parts = []
        for g in range(group):
            w = core * (count // 2) + b * group + g
            first, second = own[w], other[w]
            parts.append(jnp.where(mine, first, second))
            parts.append(jnp.where(mine, second, first))
        data = jnp.concatenate(parts, axis=0)
        value = mul3(split(bases[index[0, core * blocks + b]]), split(data))
        rotated[b * order : (b + 1) * order, :] = value
    rot_high[...], rot_low[...] = split(rotated[...].T)
    sk_high[core], sk_low[core] = split(own[...].reshape(count * lows, rank))
    sk_high[1 - core], sk_low[1 - core] = split(other[...].reshape(count * lows, rank))


def rotate_sketch(where, index, own, other, bases):
    count, lows, rank = own.shape
    rows = count * lows
    vmem = pl.BlockSpec(memory_space=pltpu.VMEM)
    smem = pl.BlockSpec(memory_space=pltpu.SMEM)
    return pl.pallas_call(
        rotate_kernel,
        out_shape=(
            jax.ShapeDtypeStruct((2, rows, rank), BF16),
            jax.ShapeDtypeStruct((2, rows, rank), BF16),
            jax.ShapeDtypeStruct((rank, rows), BF16),
            jax.ShapeDtypeStruct((rank, rows), BF16),
        ),
        in_specs=[smem, smem, vmem, vmem, vmem],
        out_specs=(vmem, vmem, vmem, vmem),
        scratch_shapes=[pltpu.VMEM((rows, rank), F32)],
        compiler_params=params(12),
        name="rotate",
    )(where, index, own, other, bases)


def frobenius(mat):
    return jnp.sqrt(jnp.sum(jnp.sum(mat * mat, axis=0, keepdims=True), axis=1, keepdims=True))


def eye(n):
    return (
        lax.broadcasted_iota(jnp.int32, (n, n), 0) == lax.broadcasted_iota(jnp.int32, (n, n), 1)
    ).astype(F32)


def newton(mat, value):
    t = mat
    held = None
    for step in range(NS_ITERS):
        last = step == NS_ITERS - 1
        right = split(t)
        if step == 0:
            once = 1.5 * t - 0.5 * mul3(right, right)
            held = 1.5 * eye(t.shape[0]) - 0.5 * t if value is None else once
        else:
            if not last:
                once = 1.5 * t - 0.5 * mul3(right, right)
            held = 1.5 * held - 0.5 * mul3(split(held), right)
        if not last:
            t = 1.5 * once - 0.5 * mul3(split(once), right)
    return held


def output_kernel(
    where, mine, other, table, sk_high, sk_low, rot_high, rot_low, new, weights, proj
):
    rank = proj.shape[0]
    halves = sk_high.shape[0]
    width = rank // halves
    first = pl.ds(pl.multiple_of(where[0] * width, width), width)
    second = pl.ds(pl.multiple_of((1 - where[0]) * width, width), width)
    for j in range(mine.shape[1]):
        cols = slice(j * 128, (j + 1) * 128)
        proj[first, cols] = mine[:, j].reshape(width, 128)
        proj[second, cols] = other[:, j].reshape(width, 128)
    p = split(proj[...])
    gram = dot(p[0], table[...]) + dot(p[1], table[...])
    inverse = newton(gram / (frobenius(gram) + 1e-6), None)
    inv = split(inverse)
    coeff = split(mul3(inv, p))
    core = mul3(coeff, coeff, NT)
    shift = frobenius(core) + 1e-6
    root = split(newton(core / shift, "approx"))
    scale = jnp.sqrt(shift)
    mixing = scale * mul3(inv, root)
    turned = split(scale * mul3(root, inv))
    own = jnp.where(where[0] == 0, mixing[:, :width], mixing[:, width:])
    own = split(own)
    rot = mul3(turned, (rot_high[...], rot_low[...]))
    weights[...] = jnp.sum(rot * rot, axis=0, keepdims=True) / rank
    for c in range(halves):
        value = mul3((sk_high[c], sk_low[c]), own)
        new[:, c] = value.reshape(new.shape[0], new.shape[2], width)


def outputs(where, mine, other, table, sk_high, sk_low, rot_high, rot_low, lows):
    halves, rows, rank = sk_high.shape
    vmem = pl.BlockSpec(memory_space=pltpu.VMEM)
    smem = pl.BlockSpec(memory_space=pltpu.SMEM)
    return pl.pallas_call(
        output_kernel,
        out_shape=(
            jax.ShapeDtypeStruct((rows // lows, halves, lows, rank // halves), F32),
            jax.ShapeDtypeStruct((1, rows), F32),
        ),
        in_specs=[smem] + [vmem] * 7,
        out_specs=(vmem, vmem),
        scratch_shapes=[pltpu.VMEM((rank, table.shape[0]), F32)],
        compiler_params=params(20),
        name="outputs",
    )(where, mine, other, table, sk_high, sk_low, rot_high, rot_low)


def sketch_table(sketch_perm, rank):
    target = sketch_perm % rank
    sign = 1.0 - 2.0 * (sketch_perm // rank % 2).astype(F32)
    hit = target[:, None] == jnp.arange(rank, dtype=jnp.int32)[None, :]
    return jnp.where(hit, sign[:, None], jnp.zeros((), F32)).astype(BF16)


def swap(value):
    return lax.ppermute(value, "cols", [(0, 1), (1, 0)])


def per_device(factor, gates, gate_layout, jump_masks, jump_rates, sketch_perm, bases, basis_index):
    rows, width = factor.shape
    count = lax.axis_size("wide")
    rank = width * lax.axis_size("cols")
    where = lax.axis_index("cols").astype(jnp.int32).reshape(1)
    kept, sent = apply_gates(where, gates, gate_layout, factor, count)
    pieces = join_columns(where, swap(sent), kept)
    moved = lax.all_to_all(pieces, "wide", split_axis=0, concat_axis=0, tiled=True)
    table = sketch_table(sketch_perm, rank)
    sketch, keep, send = stack_products(where, jump_masks, jump_rates, moved, table)
    part = keep + swap(send)
    total, other = sum_wide(part, swap(sketch))
    turned = rotate_sketch(where, basis_index, sketch, other, bases)
    total, turned = lax.optimization_barrier((total, turned))
    new, weights = outputs(where, total, swap(total), table, *turned, moved.shape[2])
    return new.reshape(rows, width), weights


def solution(mesh):
    return jax.shard_map(
        per_device,
        mesh=mesh,
        in_specs=(P("wide", "cols"), P(), P("wide"), P(), P(), P(), P(), P("wide", None)),
        out_specs=(P("wide", "cols"), P("wide", "cols")),
        check_vma=False,
    )
```

```python
import jax
import jax.numpy as jnp
from jax import lax
from jax.experimental import pallas as pl
from jax.experimental.pallas import tpu as pltpu
from jax.sharding import PartitionSpec as P

NS_ITERS = 7
F32 = jnp.float32
BF16 = jnp.bfloat16
NN = (((1,), (0,)), ((), ()))
NT = (((1,), (1,)), ((), ()))


def split(x):
    hi = x.astype(BF16)
    return hi, (x - hi.astype(F32)).astype(BF16)


def dot(a, b, dims=NN):
    return lax.dot_general(a, b, dims, preferred_element_type=F32)


def halves_of(x):
    half = x.shape[0] // 2
    return x[:half], x[half:]


def mul3(a, b, dims=NN):
    left = jnp.concatenate([a[0], a[1], a[0]], axis=dims[0][0][0])
    right = jnp.concatenate([b[0], b[0], b[1]], axis=dims[0][1][0])
    return jnp.concatenate([dot(rows, right, dims) for rows in halves_of(left)], axis=0)


def params(mib):
    return pltpu.CompilerParams(vmem_limit_bytes=mib << 20)


def gate_kernel(order, layout, gates, factor, out, mats, source, result, sems):
    steps = sems.shape[1] - 1
    chunk = factor.shape[0] // steps
    width = factor.shape[1]
    rows = [pl.ds(i * chunk, chunk) for i in range(steps)]
    first = pltpu.make_async_copy(gates, mats, sems.at[0, steps])
    first.start()
    arrive = []
    leave = []
    for i in range(steps):
        arrive.append(pltpu.make_async_copy(factor.at[rows[i]], source.at[rows[i]], sems.at[0, i]))
        arrive[i].start()
        leave.append(pltpu.make_async_copy(result.at[rows[i]], out.at[rows[i]], sems.at[1, i]))
    first.wait()
    for i in range(steps):
        arrive[i].wait()
        for b in range(i * chunk // order, (i + 1) * chunk // order):
            block = slice(b * order, (b + 1) * order)
            high, low = split(source[block, :])
            left = jnp.concatenate(split(mats[layout[b]]), axis=1)
            right = jnp.concatenate(
                [
                    jnp.concatenate([high, low], axis=1),
                    jnp.concatenate([high, jnp.zeros_like(high)], axis=1),
                ],
                axis=0,
            )
            both = dot(left, right)
            result[block, :] = both[:, :width] + both[:, width:]
        leave[i].start()
    for copy in leave:
        copy.wait()


def apply_gates(gates, layout, factor):
    order = gates.shape[1]
    away = pl.BlockSpec(memory_space=pltpu.HBM)
    steps = 4
    return pl.pallas_call(
        lambda *refs: gate_kernel(order, *refs),
        out_shape=jax.ShapeDtypeStruct(factor.shape, F32),
        in_specs=[pl.BlockSpec(memory_space=pltpu.SMEM), away, away],
        out_specs=away,
        scratch_shapes=[
            pltpu.VMEM(gates.shape, F32),
            pltpu.VMEM(factor.shape, F32),
            pltpu.VMEM(factor.shape, F32),
            pltpu.SemaphoreType.DMA((2, steps + 1)),
        ],
        compiler_params=params(8),
        name="gates",
    )(layout, gates, factor)


def stack_kernel(where, masks, rates, moved, table, sketch, keep, send, high, low):
    count, halves, lows, width = moved.shape
    rank = halves * width
    jumps = masks.shape[0]
    total = rates[0]
    for k in range(1, jumps):
        total = total + rates[k]
    coefs = [jnp.full((2 * lows, width), 1.0 - 0.5 * total, F32)]
    for k in range(jumps):
        coefs.append(jnp.sqrt(jnp.full((2 * lows, width), rates[k], F32)))

    value = [jnp.zeros((count * lows // 2, rank), F32)] * 2
    for k in range(jumps + 1):
        flip = 0 if k == 0 else masks[k - 1]
        cols = slice(k * rank, (k + 1) * rank)
        for p in range(count // 2):
            first, second = (2 * p) ^ flip, (2 * p + 1) ^ flip
            rows = slice(p * 2 * lows, (p + 1) * 2 * lows)
            for c in range(halves):
                pair = coefs[k] * jnp.concatenate([moved[first, c], moved[second, c]], axis=0)
                part = slice(k * rank + c * width, k * rank + (c + 1) * width)
                high[rows, part], low[rows, part] = split(pair)
        left = jnp.concatenate([high[:, cols], low[:, cols]], axis=1)
        right = jnp.concatenate([table[cols, :]] * 2, axis=0)
        value = [v + dot(rows, right) for v, rows in zip(value, halves_of(left))]
    value = jnp.concatenate(value, axis=0)
    sketch[...] = value.reshape(sketch.shape)
    left = split(value.T)
    mine = where[0] == 0
    half = rank // 2
    for k in range(jumps + 1):
        cols = slice(k * rank, (k + 1) * rank)
        part = mul3(left, (high[:, cols], low[:, cols]))
        for j in range(rank // 128):
            tiles = part[:, j * 128 : (j + 1) * 128]
            top = tiles[:half].reshape(half // 8, 8, 128)
            bottom = tiles[half:].reshape(half // 8, 8, 128)
            keep[:, k * (rank // 128) + j] = jnp.where(mine, top, bottom)
            send[:, k * (rank // 128) + j] = jnp.where(mine, bottom, top)


def stack_products(where, masks, rates, moved, table):
    count, halves, lows, width = moved.shape
    rank = halves * width
    columns = table.shape[0]
    vmem = pl.BlockSpec(memory_space=pltpu.VMEM)
    smem = pl.BlockSpec(memory_space=pltpu.SMEM)
    half = jax.ShapeDtypeStruct((rank // 16, columns // 128, 8, 128), F32)
    return pl.pallas_call(
        stack_kernel,
        out_shape=(jax.ShapeDtypeStruct((count, lows, rank), F32), half, half),
        in_specs=[smem, smem, smem, vmem, vmem],
        out_specs=(vmem, vmem, vmem),
        scratch_shapes=[pltpu.VMEM((count * lows, columns), BF16)] * 2,
        compiler_params=params(20),
        name="stack",
    )(where, masks, rates, moved, table)


SIDES = (4, 8, 4)


def groups(count):
    ny, nz, nx = SIDES
    assert ny * nz * nx == count
    at = lambda y, z, x: (y * nz + z) * nx + x
    planes = [[at(y, z, x) for y in range(ny) for x in range(nx)] for z in range(nz)]
    lines = [[at(y, z, x) for z in range(nz)] for y in range(ny) for x in range(nx)]
    return planes, lines


def spread_kernel(parts, out):
    out[...] = jnp.broadcast_to(jnp.sum(parts[...], axis=0, keepdims=True), out.shape)


def sum_and_spread(parts, copies):
    vmem = pl.BlockSpec(memory_space=pltpu.VMEM)
    return pl.pallas_call(
        spread_kernel,
        out_shape=jax.ShapeDtypeStruct((copies,) + parts.shape[1:], F32),
        in_specs=[vmem],
        out_specs=vmem,
        compiler_params=params(4),
        name="spread",
    )(parts)


def exchange(pieces, members):
    return lax.all_to_all(
        pieces, "wide", split_axis=0, concat_axis=0, axis_index_groups=members, tiled=True
    )


def sum_wide(part, beside):
    planes, lines = groups(lax.axis_size("wide"))
    assert len(planes[0]) == part.shape[0]
    pieces = exchange(part, planes)
    pieces, beside = lax.optimization_barrier((pieces, beside))
    pieces = exchange(sum_and_spread(pieces, len(lines[0])), lines)
    return exchange(sum_and_spread(pieces, len(planes[0])), planes), beside


def rotate_kernel(where, index, own, other, bases, sk, rot, rotated, sk_near, rot_near, sems):
    count, lows, rank = own.shape
    order = bases.shape[1]
    group = order // (2 * lows)
    blocks = rotated.shape[0] // order
    core = where[0]
    mine = core == 0
    for part, value in enumerate(split(own[...].reshape(count * lows, rank))):
        sk_near[part, core] = value
    for part, value in enumerate(split(other[...].reshape(count * lows, rank))):
        sk_near[part, 1 - core] = value
    leave = pltpu.make_async_copy(sk_near, sk, sems.at[0])
    leave.start()
    for b in range(blocks):
        parts = []
        for g in range(group):
            w = core * (count // 2) + b * group + g
            first, second = own[w], other[w]
            parts.append(jnp.where(mine, first, second))
            parts.append(jnp.where(mine, second, first))
        data = jnp.concatenate(parts, axis=0)
        value = mul3(split(bases[index[0, core * blocks + b]]), split(data))
        rotated[b * order : (b + 1) * order, :] = value
    rot_near[0], rot_near[1] = split(rotated[...].T)
    last = pltpu.make_async_copy(rot_near, rot, sems.at[1])
    last.start()
    leave.wait()
    last.wait()


def rotate_sketch(where, index, own, other, bases):
    count, lows, rank = own.shape
    rows = count * lows
    vmem = pl.BlockSpec(memory_space=pltpu.VMEM)
    smem = pl.BlockSpec(memory_space=pltpu.SMEM)
    away = pl.BlockSpec(memory_space=pltpu.HBM)
    shapes = ((2, 2, rows, rank), (2, rank, rows))
    return pl.pallas_call(
        rotate_kernel,
        out_shape=tuple(jax.ShapeDtypeStruct(shape, BF16) for shape in shapes),
        in_specs=[smem, smem, vmem, vmem, vmem],
        out_specs=(away, away),
        scratch_shapes=[pltpu.VMEM((rows, rank), F32)]
        + [pltpu.VMEM(shape, BF16) for shape in shapes]
        + [pltpu.SemaphoreType.DMA((2,))],
        compiler_params=params(16),
        name="rotate",
    )(where, index, own, other, bases)


def frobenius(mat):
    return jnp.sqrt(jnp.sum(jnp.sum(mat * mat, axis=0, keepdims=True), axis=1, keepdims=True))


def eye(n):
    return (
        lax.broadcasted_iota(jnp.int32, (n, n), 0) == lax.broadcasted_iota(jnp.int32, (n, n), 1)
    ).astype(F32)


def newton(mat, value):
    t = mat
    held = None
    for step in range(NS_ITERS):
        last = step == NS_ITERS - 1
        right = split(t)
        if step == 0:
            once = 1.5 * t - 0.5 * mul3(right, right)
            held = 1.5 * eye(t.shape[0]) - 0.5 * t if value is None else once
        else:
            if not last:
                once = 1.5 * t - 0.5 * mul3(right, right)
            held = 1.5 * held - 0.5 * mul3(split(held), right)
        if not last:
            t = 1.5 * once - 0.5 * mul3(split(once), right)
    return held


def output_kernel(where, mine, other, table, sk, rot, new, weights, proj, sk_near, rot_near, sems):
    rank = proj.shape[0]
    halves = sk.shape[1]
    width = rank // halves
    copies = [
        pltpu.make_async_copy(rot, rot_near, sems.at[0]),
        pltpu.make_async_copy(sk, sk_near, sems.at[1]),
    ]
    for copy in copies:
        copy.start()
    first = pl.ds(pl.multiple_of(where[0] * width, width), width)
    second = pl.ds(pl.multiple_of((1 - where[0]) * width, width), width)
    for j in range(mine.shape[1]):
        cols = slice(j * 128, (j + 1) * 128)
        proj[first, cols] = mine[:, j].reshape(width, 128)
        proj[second, cols] = other[:, j].reshape(width, 128)
    p = split(proj[...])
    left = jnp.concatenate(p, axis=1)
    right = jnp.concatenate([table[...]] * 2, axis=0)
    gram = jnp.concatenate([dot(rows, right) for rows in halves_of(left)], axis=0)
    inverse = newton(gram / (frobenius(gram) + 1e-6), None)
    inv = split(inverse)
    coeff = split(mul3(inv, p))
    core = mul3(coeff, coeff, NT)
    shift = frobenius(core) + 1e-6
    root = split(newton(core / shift, "approx"))
    scale = jnp.sqrt(shift)
    mixing = scale * mul3(inv, root)
    turned = split(scale * mul3(root, inv))
    own = split(jnp.where(where[0] == 0, mixing[:, :width], mixing[:, width:]))
    copies[1].wait()
    for c in range(halves):
        value = mul3((sk_near[0, c], sk_near[1, c]), own)
        new[:, c] = value.reshape(new.shape[0], new.shape[2], width)
    copies[0].wait()
    turn = mul3(turned, (rot_near[0], rot_near[1]))
    weights[...] = jnp.sum(turn * turn, axis=0, keepdims=True) / rank


def outputs(where, mine, other, table, sk, rot, lows):
    halves, rows, rank = sk.shape[1:]
    vmem = pl.BlockSpec(memory_space=pltpu.VMEM)
    smem = pl.BlockSpec(memory_space=pltpu.SMEM)
    away = pl.BlockSpec(memory_space=pltpu.HBM)
    return pl.pallas_call(
        output_kernel,
        out_shape=(
            jax.ShapeDtypeStruct((rows // lows, halves, lows, rank // halves), F32),
            jax.ShapeDtypeStruct((1, rows), F32),
        ),
        in_specs=[smem] + [vmem] * 3 + [away] * 2,
        out_specs=(vmem, vmem),
        scratch_shapes=[
            pltpu.VMEM((rank, table.shape[0]), F32),
            pltpu.VMEM(sk.shape, BF16),
            pltpu.VMEM(rot.shape, BF16),
            pltpu.SemaphoreType.DMA((2,)),
        ],
        compiler_params=params(20),
        name="outputs",
    )(where, mine, other, table, sk, rot)


def sketch_table(sketch_perm, rank):
    target = sketch_perm % rank
    sign = 1.0 - 2.0 * (sketch_perm // rank % 2).astype(F32)
    hit = target[:, None] == jnp.arange(rank, dtype=jnp.int32)[None, :]
    return jnp.where(hit, sign[:, None], jnp.zeros((), F32)).astype(BF16)


def swap(value):
    return lax.ppermute(value, "cols", [(0, 1), (1, 0)])


def per_device(factor, gates, gate_layout, jump_masks, jump_rates, sketch_perm, bases, basis_index):
    rows, width = factor.shape
    count = lax.axis_size("wide")
    rank = width * lax.axis_size("cols")
    where = lax.axis_index("cols").astype(jnp.int32).reshape(1)
    gated = apply_gates(gates, gate_layout, factor).reshape(2 * count, -1, width)
    moved = lax.all_to_all(gated, ("wide", "cols"), split_axis=0, concat_axis=0, tiled=True)
    moved = moved.reshape(count, 2, -1, width)
    table = sketch_table(sketch_perm, rank)
    sketch, keep, send = stack_products(where, jump_masks, jump_rates, moved, table)
    part = keep + swap(send)
    part, sketch = lax.optimization_barrier((part, sketch))
    total, other = sum_wide(part, swap(sketch))
    turned = rotate_sketch(where, basis_index, sketch, other, bases)
    total, turned = lax.optimization_barrier((total, turned))
    new, weights = outputs(where, total, swap(total), table, *turned, moved.shape[2])
    return new.reshape(rows, width), weights


def solution(mesh):
    return jax.shard_map(
        per_device,
        mesh=mesh,
        in_specs=(P("wide", "cols"), P(), P("wide"), P(), P(), P(), P(), P("wide", None)),
        out_specs=(P("wide", "cols"), P("wide", "cols")),
        check_vma=False,
    )
```

```python
import jax
import jax.numpy as jnp
from jax import lax
from jax.experimental import pallas as pl
from jax.experimental.pallas import tpu as pltpu
from jax.sharding import PartitionSpec as P

NS_ITERS = 7
F32 = jnp.float32
BF16 = jnp.bfloat16
NN = (((1,), (0,)), ((), ()))
NT = (((1,), (1,)), ((), ()))


def split(x):
    hi = x.astype(BF16)
    return hi, (x - hi.astype(F32)).astype(BF16)


def dot(a, b, dims=NN):
    return lax.dot_general(a, b, dims, preferred_element_type=F32)


def halves_of(x):
    half = x.shape[0] // 2
    return x[:half], x[half:]


def mul3(a, b, dims=NN):
    left = jnp.concatenate([a[0], a[1], a[0]], axis=dims[0][0][0])
    right = jnp.concatenate([b[0], b[0], b[1]], axis=dims[0][1][0])
    return jnp.concatenate([dot(rows, right, dims) for rows in halves_of(left)], axis=0)


WHOLE = 60


def params(mib):
    return pltpu.CompilerParams(vmem_limit_bytes=int(mib * 2**20))


def gate_kernel(order, layout, gates, factor, out, mats, source, result, sems):
    steps = sems.shape[1] - 1
    chunk = factor.shape[0] // steps
    width = factor.shape[1]
    rows = [pl.ds(i * chunk, chunk) for i in range(steps)]
    first = pltpu.make_async_copy(gates, mats, sems.at[0, steps])
    first.start()
    arrive = []
    leave = []
    for i in range(steps):
        arrive.append(pltpu.make_async_copy(factor.at[rows[i]], source.at[rows[i]], sems.at[0, i]))
        arrive[i].start()
        leave.append(pltpu.make_async_copy(result.at[rows[i]], out.at[rows[i]], sems.at[1, i]))
    first.wait()
    for i in range(steps):
        arrive[i].wait()
        for b in range(i * chunk // order, (i + 1) * chunk // order):
            block = slice(b * order, (b + 1) * order)
            high, low = split(source[block, :])
            left = jnp.concatenate(split(mats[layout[b]]), axis=1)
            right = jnp.concatenate(
                [
                    jnp.concatenate([high, low], axis=1),
                    jnp.concatenate([high, jnp.zeros_like(high)], axis=1),
                ],
                axis=0,
            )
            both = dot(left, right)
            result[block, :] = both[:, :width] + both[:, width:]
        leave[i].start()
    for copy in leave:
        copy.wait()


def apply_gates(gates, layout, factor):
    order = gates.shape[1]
    away = pl.BlockSpec(memory_space=pltpu.HBM)
    steps = 4
    return pl.pallas_call(
        lambda *refs: gate_kernel(order, *refs),
        out_shape=jax.ShapeDtypeStruct(factor.shape, F32),
        in_specs=[pl.BlockSpec(memory_space=pltpu.SMEM), away, away],
        out_specs=away,
        scratch_shapes=[
            pltpu.VMEM(gates.shape, F32),
            pltpu.VMEM(factor.shape, F32),
            pltpu.VMEM(factor.shape, F32),
            pltpu.SemaphoreType.DMA((2, steps + 1)),
        ],
        compiler_params=params(WHOLE),
        name="gates",
    )(layout, gates, factor)


def stack_kernel(where, masks, rates, moved, table, sketch, keep, send, high, low):
    count, halves, lows, width = moved.shape
    rank = halves * width
    jumps = masks.shape[0]
    total = rates[0]
    for k in range(1, jumps):
        total = total + rates[k]
    coefs = [jnp.full((2 * lows, width), 1.0 - 0.5 * total, F32)]
    for k in range(jumps):
        coefs.append(jnp.sqrt(jnp.full((2 * lows, width), rates[k], F32)))

    value = [jnp.zeros((count * lows // 2, rank), F32)] * 2
    for k in range(jumps + 1):
        flip = 0 if k == 0 else masks[k - 1]
        cols = slice(k * rank, (k + 1) * rank)
        for p in range(count // 2):
            first, second = (2 * p) ^ flip, (2 * p + 1) ^ flip
            rows = slice(p * 2 * lows, (p + 1) * 2 * lows)
            for c in range(halves):
                pair = coefs[k] * jnp.concatenate([moved[first, c], moved[second, c]], axis=0)
                part = slice(k * rank + c * width, k * rank + (c + 1) * width)
                high[rows, part], low[rows, part] = split(pair)
        left = jnp.concatenate([high[:, cols], low[:, cols]], axis=1)
        right = jnp.concatenate([table[cols, :]] * 2, axis=0)
        value = [v + dot(rows, right) for v, rows in zip(value, halves_of(left))]
    value = jnp.concatenate(value, axis=0)
    sketch[...] = value.reshape(sketch.shape)
    left = split(value.T)
    mine = where[0] == 0
    half = rank // 2
    for k in range(jumps + 1):
        cols = slice(k * rank, (k + 1) * rank)
        part = mul3(left, (high[:, cols], low[:, cols]))
        for j in range(rank // 128):
            tiles = part[:, j * 128 : (j + 1) * 128]
            top = tiles[:half].reshape(half // 8, 8, 128)
            bottom = tiles[half:].reshape(half // 8, 8, 128)
            keep[:, k * (rank // 128) + j] = jnp.where(mine, top, bottom)
            send[:, k * (rank // 128) + j] = jnp.where(mine, bottom, top)


def stack_products(where, masks, rates, moved, table):
    count, halves, lows, width = moved.shape
    rank = halves * width
    columns = table.shape[0]
    vmem = pl.BlockSpec(memory_space=pltpu.VMEM)
    smem = pl.BlockSpec(memory_space=pltpu.SMEM)
    half = jax.ShapeDtypeStruct((rank // 16, columns // 128, 8, 128), F32)
    return pl.pallas_call(
        stack_kernel,
        out_shape=(jax.ShapeDtypeStruct((count, lows, rank), F32), half, half),
        in_specs=[smem, smem, smem, vmem, vmem],
        out_specs=(vmem, vmem, vmem),
        scratch_shapes=[pltpu.VMEM((count * lows, columns), BF16)] * 2,
        compiler_params=params(20),
        name="stack",
    )(where, masks, rates, moved, table)


SIDES = (4, 8, 4)


def groups(count):
    ny, nz, nx = SIDES
    assert ny * nz * nx == count
    at = lambda y, z, x: (y * nz + z) * nx + x
    planes = [[at(y, z, x) for y in range(ny) for x in range(nx)] for z in range(nz)]
    lines = [[at(y, z, x) for z in range(nz)] for y in range(ny) for x in range(nx)]
    return planes, lines


def spread_kernel(parts, out):
    out[...] = jnp.broadcast_to(jnp.sum(parts[...], axis=0, keepdims=True), out.shape)


def sum_and_spread(parts, copies):
    vmem = pl.BlockSpec(memory_space=pltpu.VMEM)
    return pl.pallas_call(
        spread_kernel,
        out_shape=jax.ShapeDtypeStruct((copies,) + parts.shape[1:], F32),
        in_specs=[vmem],
        out_specs=vmem,
        compiler_params=params(4),
        name="spread",
    )(parts)


def exchange(pieces, members):
    return lax.all_to_all(
        pieces, "wide", split_axis=0, concat_axis=0, axis_index_groups=members, tiled=True
    )


def sum_wide(part, beside):
    planes, lines = groups(lax.axis_size("wide"))
    assert len(planes[0]) == part.shape[0]
    pieces = exchange(part, planes)
    pieces, beside = lax.optimization_barrier((pieces, beside))
    pieces = exchange(sum_and_spread(pieces, len(lines[0])), lines)
    return exchange(sum_and_spread(pieces, len(planes[0])), planes), beside


PADDED = 16


def rotate_kernel(
    where, index, own_away, other_away, mats_away, kept,
    own, other, mats, rotated, near, sems,
):
    count, lows, rank = own.shape
    order = mats.shape[1]
    group = order // (2 * lows)
    blocks = rotated.shape[0] // order
    core = where[0]
    mine = core == 0
    arrive = [
        pltpu.make_async_copy(own_away, own, sems.at[0]),
        pltpu.make_async_copy(other_away, other, sems.at[1]),
        pltpu.make_async_copy(mats_away, mats, sems.at[2]),
    ]
    for copy in arrive:
        copy.start()
    for copy in arrive:
        copy.wait()
    for part, value in enumerate(split(own[...].reshape(count * lows, rank))):
        near[part, core] = value
    for part, value in enumerate(split(other[...].reshape(count * lows, rank))):
        near[part, 1 - core] = value
    leave = pltpu.make_async_copy(near.at[:, :2], kept.at[:, :2], sems.at[3])
    leave.start()
    for b in range(blocks):
        parts = []
        for g in range(group):
            w = core * (count // 2) + b * group + g
            first, second = own[w], other[w]
            parts.append(jnp.where(mine, first, second))
            parts.append(jnp.where(mine, second, first))
        data = jnp.concatenate(parts, axis=0)
        value = mul3(split(mats[index[0, core * blocks + b]]), split(data))
        rotated[b * order : (b + 1) * order, :] = value
    for q in range(rotated.shape[0] // rank):
        rows = slice(q * rank, (q + 1) * rank)
        for part, value in enumerate(split(rotated[rows, :].T)):
            near[part, 2, rows] = value
    last = pltpu.make_async_copy(near.at[:, 2], kept.at[:, 2], sems.at[4])
    last.start()
    leave.wait()
    last.wait()


def rotate_sketch(where, index, own, other, bases):
    count, lows, rank = own.shape
    rows = count * lows
    smem = pl.BlockSpec(memory_space=pltpu.SMEM)
    away = pl.BlockSpec(memory_space=pl.ANY)
    return pl.pallas_call(
        rotate_kernel,
        out_shape=jax.ShapeDtypeStruct((2, PADDED, rows, rank), BF16),
        in_specs=[smem, smem, away, away, away],
        out_specs=away,
        scratch_shapes=[
            pltpu.VMEM(own.shape, F32),
            pltpu.VMEM(own.shape, F32),
            pltpu.VMEM(bases.shape, F32),
            pltpu.VMEM((rows, rank), F32),
            pltpu.VMEM((2, 3, rows, rank), BF16),
            pltpu.SemaphoreType.DMA((5,)),
        ],
        compiler_params=params(WHOLE),
        name="rotate",
    )(where, index, own, other, bases)


def frobenius(mat):
    return jnp.sqrt(jnp.sum(jnp.sum(mat * mat, axis=0, keepdims=True), axis=1, keepdims=True))


def eye(n):
    return (
        lax.broadcasted_iota(jnp.int32, (n, n), 0) == lax.broadcasted_iota(jnp.int32, (n, n), 1)
    ).astype(F32)


def newton(mat, value):
    t = mat
    held = None
    for step in range(NS_ITERS):
        last = step == NS_ITERS - 1
        right = split(t)
        if step == 0:
            once = 1.5 * t - 0.5 * mul3(right, right)
            held = 1.5 * eye(t.shape[0]) - 0.5 * t if value is None else once
        else:
            if not last:
                once = 1.5 * t - 0.5 * mul3(right, right)
            held = 1.5 * held - 0.5 * mul3(split(held), right)
        if not last:
            t = 1.5 * once - 0.5 * mul3(split(once), right)
    return held


def output_kernel(where, mine, other, table, away, new, weights, proj, kept, new_near, sems):
    rank = proj.shape[0]
    halves = new.shape[1]
    width = rank // halves
    fetch = pltpu.make_async_copy(away.at[:, : kept.shape[1]], kept, sems.at[2])
    fetch.start()
    first = pl.ds(pl.multiple_of(where[0] * width, width), width)
    second = pl.ds(pl.multiple_of((1 - where[0]) * width, width), width)
    for j in range(mine.shape[1]):
        cols = slice(j * 128, (j + 1) * 128)
        proj[first, cols] = mine[:, j].reshape(width, 128)
        proj[second, cols] = other[:, j].reshape(width, 128)
    p = split(proj[...])
    left = jnp.concatenate(p, axis=1)
    right = jnp.concatenate([table[...]] * 2, axis=0)
    gram = jnp.concatenate([dot(part, right) for part in halves_of(left)], axis=0)
    inverse = newton(gram / (frobenius(gram) + 1e-6), None)
    inv = split(inverse)
    coeff = split(mul3(inv, p))
    core = mul3(coeff, coeff, NT)
    shift = frobenius(core) + 1e-6
    root = split(newton(core / shift, "approx"))
    scale = jnp.sqrt(shift)
    mixing = scale * mul3(inv, root)
    turned = split(scale * mul3(root, inv))
    high, low = split(jnp.where(where[0] == 0, mixing[:, :width], mixing[:, width:]))
    right = jnp.concatenate(
        [
            jnp.concatenate([high, low], axis=1),
            jnp.concatenate([high, jnp.zeros_like(high)], axis=1),
        ],
        axis=0,
    )
    fetch.wait()
    leave = []
    for c in range(halves):
        left = jnp.concatenate([kept[0, c], kept[1, c]], axis=1)
        both = jnp.concatenate([dot(part, right) for part in halves_of(left)], axis=0)
        value = both[:, :width] + both[:, width:]
        new_near[c] = value.reshape(new_near.shape[1:])
        leave.append(pltpu.make_async_copy(new_near.at[c], new.at[:, c], sems.at[c]))
        leave[c].start()
    for q in range(kept.shape[2] // rank):
        rows = slice(q * rank, (q + 1) * rank)
        turn = mul3(turned, (kept[0, 2, rows], kept[1, 2, rows]))
        weights[:, rows] = jnp.sum(turn * turn, axis=0, keepdims=True) / rank
    for copy in leave:
        copy.wait()


def outputs(where, mine, other, table, kept, lows):
    rows, rank = kept.shape[2:]
    width = rank // 2
    smem = pl.BlockSpec(memory_space=pltpu.SMEM)
    vmem = pl.BlockSpec(memory_space=pltpu.VMEM)
    away = pl.BlockSpec(memory_space=pl.ANY)
    return pl.pallas_call(
        output_kernel,
        out_shape=(
            jax.ShapeDtypeStruct((rows // lows, 2, lows, width), F32),
            jax.ShapeDtypeStruct((1, rows), F32),
        ),
        in_specs=[smem] + [vmem] * 3 + [away],
        out_specs=(away, vmem),
        scratch_shapes=[
            pltpu.VMEM((rank, table.shape[0]), F32),
            pltpu.VMEM((2, 3, rows, rank), BF16),
            pltpu.VMEM((2, rows // lows, lows, width), F32),
            pltpu.SemaphoreType.DMA((3,)),
        ],
        compiler_params=params(48),
        name="outputs",
    )(where, mine, other, table, kept)


def sketch_table(sketch_perm, rank):
    target = sketch_perm % rank
    sign = 1.0 - 2.0 * (sketch_perm // rank % 2).astype(F32)
    hit = target[:, None] == jnp.arange(rank, dtype=jnp.int32)[None, :]
    return jnp.where(hit, sign[:, None], jnp.zeros((), F32)).astype(BF16)


def swap(value):
    return lax.ppermute(value, "cols", [(0, 1), (1, 0)])


def per_device(factor, gates, gate_layout, jump_masks, jump_rates, sketch_perm, bases, basis_index):
    rows, width = factor.shape
    count = lax.axis_size("wide")
    rank = width * lax.axis_size("cols")
    where = lax.axis_index("cols").astype(jnp.int32).reshape(1)
    gated = apply_gates(gates, gate_layout, factor).reshape(2 * count, -1, width)
    moved = lax.all_to_all(gated, ("wide", "cols"), split_axis=0, concat_axis=0, tiled=True)
    moved = moved.reshape(count, 2, -1, width)
    table = sketch_table(sketch_perm, rank)
    sketch, keep, send = stack_products(where, jump_masks, jump_rates, moved, table)
    part = keep + swap(send)
    part, sketch = lax.optimization_barrier((part, sketch))
    total, other = sum_wide(part, swap(sketch))
    turned = rotate_sketch(where, basis_index, sketch, other, bases)
    total, turned = lax.optimization_barrier((total, turned))
    new, weights = outputs(where, total, swap(total), table, turned, moved.shape[2])
    return new.reshape(rows, width), weights


def solution(mesh):
    return jax.shard_map(
        per_device,
        mesh=mesh,
        in_specs=(P("wide", "cols"), P(), P("wide"), P(), P(), P(), P(), P("wide", None)),
        out_specs=(P("wide", "cols"), P("wide", "cols")),
        check_vma=False,
    )
```

```python
import jax
import jax.numpy as jnp
from jax import lax
from jax.experimental import pallas as pl
from jax.experimental.pallas import tpu as pltpu
from jax.sharding import PartitionSpec as P

NS_ITERS = 7
F32 = jnp.float32
BF16 = jnp.bfloat16
NN = (((1,), (0,)), ((), ()))
NT = (((1,), (1,)), ((), ()))


def split(x):
    hi = x.astype(BF16)
    return hi, (x - hi.astype(F32)).astype(BF16)


def dot(a, b, dims=NN):
    return lax.dot_general(a, b, dims, preferred_element_type=F32)


def halves_of(x):
    half = x.shape[0] // 2
    return x[:half], x[half:]


def mul3(a, b, dims=NN):
    left = jnp.concatenate([a[0], a[1], a[0]], axis=dims[0][0][0])
    right = jnp.concatenate([b[0], b[0], b[1]], axis=dims[0][1][0])
    return jnp.concatenate([dot(rows, right, dims) for rows in halves_of(left)], axis=0)


WHOLE = 60


def params(mib):
    return pltpu.CompilerParams(vmem_limit_bytes=int(mib * 2**20))


def gate_kernel(order, layout, gates, factor, out, mats, source, result, sems):
    steps = sems.shape[1] - 1
    chunk = factor.shape[0] // steps
    width = factor.shape[1]
    rows = [pl.ds(i * chunk, chunk) for i in range(steps)]
    first = pltpu.make_async_copy(gates, mats, sems.at[0, steps])
    first.start()
    arrive = []
    leave = []
    for i in range(steps):
        arrive.append(pltpu.make_async_copy(factor.at[rows[i]], source.at[rows[i]], sems.at[0, i]))
        arrive[i].start()
        leave.append(pltpu.make_async_copy(result.at[rows[i]], out.at[rows[i]], sems.at[1, i]))
    first.wait()
    for i in range(steps):
        arrive[i].wait()
        for b in range(i * chunk // order, (i + 1) * chunk // order):
            block = slice(b * order, (b + 1) * order)
            high, low = split(source[block, :])
            left = jnp.concatenate(split(mats[layout[b]]), axis=1)
            right = jnp.concatenate(
                [
                    jnp.concatenate([high, low], axis=1),
                    jnp.concatenate([high, jnp.zeros_like(high)], axis=1),
                ],
                axis=0,
            )
            both = dot(left, right)
            result[block, :] = both[:, :width] + both[:, width:]
        leave[i].start()
    for copy in leave:
        copy.wait()


def apply_gates(gates, layout, factor):
    order = gates.shape[1]
    away = pl.BlockSpec(memory_space=pltpu.HBM)
    steps = 4
    return pl.pallas_call(
        lambda *refs: gate_kernel(order, *refs),
        out_shape=jax.ShapeDtypeStruct(factor.shape, F32),
        in_specs=[pl.BlockSpec(memory_space=pltpu.SMEM), away, away],
        out_specs=away,
        scratch_shapes=[
            pltpu.VMEM(gates.shape, F32),
            pltpu.VMEM(factor.shape, F32),
            pltpu.VMEM(factor.shape, F32),
            pltpu.SemaphoreType.DMA((2, steps + 1)),
        ],
        compiler_params=params(WHOLE),
        name="gates",
    )(layout, gates, factor)


def stack_kernel(where, flips, coefs, moved, table, sketch, keep, send, high, low):
    count, halves, lows, width = moved.shape
    rank = halves * width
    value = [jnp.zeros((count * lows // 2, rank), F32)] * 2
    terms = flips.shape[0]
    for k in range(terms):
        flip = flips[k]
        cols = slice(k * rank, (k + 1) * rank)
        for p in range(count // 2):
            first, second = (2 * p) ^ flip, (2 * p + 1) ^ flip
            rows = slice(p * 2 * lows, (p + 1) * 2 * lows)
            for c in range(halves):
                pair = coefs[k] * jnp.concatenate([moved[first, c], moved[second, c]], axis=0)
                part = slice(k * rank + c * width, k * rank + (c + 1) * width)
                high[rows, part], low[rows, part] = split(pair)
        left = jnp.concatenate([high[:, cols], low[:, cols]], axis=1)
        right = jnp.concatenate([table[cols, :]] * 2, axis=0)
        value = [v + dot(rows, right) for v, rows in zip(value, halves_of(left))]
    value = jnp.concatenate(value, axis=0)
    sketch[...] = value.reshape(sketch.shape)
    left = split(value.T)
    mine = where[0] == 0
    half = rank // 2
    for k in range(terms):
        cols = slice(k * rank, (k + 1) * rank)
        part = mul3(left, (high[:, cols], low[:, cols]))
        for j in range(rank // 128):
            tiles = part[:, j * 128 : (j + 1) * 128]
            top = tiles[:half].reshape(half // 8, 8, 128)
            bottom = tiles[half:].reshape(half // 8, 8, 128)
            keep[:, k * (rank // 128) + j] = jnp.where(mine, top, bottom)
            send[:, k * (rank // 128) + j] = jnp.where(mine, bottom, top)


def stack_products(where, flips, coefs, moved, table):
    count, halves, lows, width = moved.shape
    rank = halves * width
    columns = table.shape[0]
    vmem = pl.BlockSpec(memory_space=pltpu.VMEM)
    smem = pl.BlockSpec(memory_space=pltpu.SMEM)
    half = jax.ShapeDtypeStruct((rank // 16, columns // 128, 8, 128), F32)
    return pl.pallas_call(
        stack_kernel,
        out_shape=(jax.ShapeDtypeStruct((count, lows, rank), F32), half, half),
        in_specs=[smem, smem, smem, vmem, vmem],
        out_specs=(vmem, vmem, vmem),
        scratch_shapes=[pltpu.VMEM((count * lows, columns), BF16)] * 2,
        compiler_params=params(20),
        name="stack",
    )(where, flips, coefs, moved, table)


SIDES = (4, 8, 4)


def groups(count):
    ny, nz, nx = SIDES
    assert ny * nz * nx == count
    at = lambda y, z, x: (y * nz + z) * nx + x
    planes = [[at(y, z, x) for y in range(ny) for x in range(nx)] for z in range(nz)]
    lines = [[at(y, z, x) for z in range(nz)] for y in range(ny) for x in range(nx)]
    return planes, lines


def spread_kernel(parts, out):
    out[...] = jnp.broadcast_to(jnp.sum(parts[...], axis=0, keepdims=True), out.shape)


def sum_and_spread(parts, copies):
    vmem = pl.BlockSpec(memory_space=pltpu.VMEM)
    return pl.pallas_call(
        spread_kernel,
        out_shape=jax.ShapeDtypeStruct((copies,) + parts.shape[1:], F32),
        in_specs=[vmem],
        out_specs=vmem,
        compiler_params=params(4),
        name="spread",
    )(parts)


def exchange(pieces, members):
    return lax.all_to_all(
        pieces, "wide", split_axis=0, concat_axis=0, axis_index_groups=members, tiled=True
    )


def sum_wide(part, beside):
    planes, lines = groups(lax.axis_size("wide"))
    assert len(planes[0]) == part.shape[0]
    pieces = exchange(part, planes)
    pieces, beside = lax.optimization_barrier((pieces, beside))
    pieces = exchange(sum_and_spread(pieces, len(lines[0])), lines)
    return exchange(sum_and_spread(pieces, len(planes[0])), planes), beside


PADDED = 16


def rotate_kernel(
    where, index, own_away, other_away, mats_away, kept,
    own, other, mats, rotated, near, sems,
):
    count, lows, rank = own.shape
    order = mats.shape[1]
    group = order // (2 * lows)
    blocks = rotated.shape[0] // order
    core = where[0]
    mine = core == 0
    arrive = [
        pltpu.make_async_copy(own_away, own, sems.at[0]),
        pltpu.make_async_copy(other_away, other, sems.at[1]),
        pltpu.make_async_copy(mats_away, mats, sems.at[2]),
    ]
    for copy in arrive:
        copy.start()
    for copy in arrive:
        copy.wait()
    for part, value in enumerate(split(own[...].reshape(count * lows, rank))):
        near[part, core] = value
    for part, value in enumerate(split(other[...].reshape(count * lows, rank))):
        near[part, 1 - core] = value
    leave = pltpu.make_async_copy(near.at[:, :2], kept.at[:, :2], sems.at[3])
    leave.start()
    for b in range(blocks):
        parts = []
        for g in range(group):
            w = core * (count // 2) + b * group + g
            first, second = own[w], other[w]
            parts.append(jnp.where(mine, first, second))
            parts.append(jnp.where(mine, second, first))
        data = jnp.concatenate(parts, axis=0)
        value = mul3(split(mats[index[0, core * blocks + b]]), split(data))
        rotated[b * order : (b + 1) * order, :] = value
    for q in range(rotated.shape[0] // rank):
        rows = slice(q * rank, (q + 1) * rank)
        for part, value in enumerate(split(rotated[rows, :].T)):
            near[part, 2, rows] = value
    last = pltpu.make_async_copy(near.at[:, 2], kept.at[:, 2], sems.at[4])
    last.start()
    leave.wait()
    last.wait()


def rotate_sketch(where, index, own, other, bases):
    count, lows, rank = own.shape
    rows = count * lows
    smem = pl.BlockSpec(memory_space=pltpu.SMEM)
    away = pl.BlockSpec(memory_space=pl.ANY)
    return pl.pallas_call(
        rotate_kernel,
        out_shape=jax.ShapeDtypeStruct((2, PADDED, rows, rank), BF16),
        in_specs=[smem, smem, away, away, away],
        out_specs=away,
        scratch_shapes=[
            pltpu.VMEM(own.shape, F32),
            pltpu.VMEM(own.shape, F32),
            pltpu.VMEM(bases.shape, F32),
            pltpu.VMEM((rows, rank), F32),
            pltpu.VMEM((2, 3, rows, rank), BF16),
            pltpu.SemaphoreType.DMA((5,)),
        ],
        compiler_params=params(WHOLE),
        name="rotate",
    )(where, index, own, other, bases)


def frobenius(mat):
    return jnp.sqrt(jnp.sum(jnp.sum(mat * mat, axis=0, keepdims=True), axis=1, keepdims=True))


def eye(n):
    return (
        lax.broadcasted_iota(jnp.int32, (n, n), 0) == lax.broadcasted_iota(jnp.int32, (n, n), 1)
    ).astype(F32)


def newton(mat, value):
    t = mat
    held = None
    for step in range(NS_ITERS):
        last = step == NS_ITERS - 1
        right = split(t)
        if step == 0:
            once = 1.5 * t - 0.5 * mul3(right, right)
            held = 1.5 * eye(t.shape[0]) - 0.5 * t if value is None else once
        else:
            if not last:
                once = 1.5 * t - 0.5 * mul3(right, right)
            held = 1.5 * held - 0.5 * mul3(split(held), right)
        if not last:
            t = 1.5 * once - 0.5 * mul3(split(once), right)
    return held


def output_kernel(where, mine, other, table, away, new, weights, proj, kept, new_near, sems):
    rank = proj.shape[0]
    halves = new.shape[1]
    width = rank // halves
    fetch = pltpu.make_async_copy(away.at[:, : kept.shape[1]], kept, sems.at[2])
    fetch.start()
    first = pl.ds(pl.multiple_of(where[0] * width, width), width)
    second = pl.ds(pl.multiple_of((1 - where[0]) * width, width), width)
    for j in range(mine.shape[1]):
        cols = slice(j * 128, (j + 1) * 128)
        proj[first, cols] = mine[:, j].reshape(width, 128)
        proj[second, cols] = other[:, j].reshape(width, 128)
    p = split(proj[...])
    left = jnp.concatenate(p, axis=1)
    right = jnp.concatenate([table[...]] * 2, axis=0)
    gram = jnp.concatenate([dot(part, right) for part in halves_of(left)], axis=0)
    inverse = newton(gram / (frobenius(gram) + 1e-6), None)
    inv = split(inverse)
    coeff = split(mul3(inv, p))
    core = mul3(coeff, coeff, NT)
    shift = frobenius(core) + 1e-6
    root = split(newton(core / shift, "approx"))
    scale = jnp.sqrt(shift)
    mixing = scale * mul3(inv, root)
    turned = split(scale * mul3(root, inv))
    high, low = split(jnp.where(where[0] == 0, mixing[:, :width], mixing[:, width:]))
    right = jnp.concatenate(
        [
            jnp.concatenate([high, low], axis=1),
            jnp.concatenate([high, jnp.zeros_like(high)], axis=1),
        ],
        axis=0,
    )
    fetch.wait()
    leave = []
    for c in range(halves):
        left = jnp.concatenate([kept[0, c], kept[1, c]], axis=1)
        both = jnp.concatenate([dot(part, right) for part in halves_of(left)], axis=0)
        value = both[:, :width] + both[:, width:]
        new_near[c] = value.reshape(new_near.shape[1:])
        leave.append(pltpu.make_async_copy(new_near.at[c], new.at[:, c], sems.at[c]))
        leave[c].start()
    for q in range(kept.shape[2] // rank):
        rows = slice(q * rank, (q + 1) * rank)
        turn = mul3(turned, (kept[0, 2, rows], kept[1, 2, rows]))
        weights[:, rows] = jnp.sum(turn * turn, axis=0, keepdims=True) / rank
    for copy in leave:
        copy.wait()


def outputs(where, mine, other, table, kept, lows):
    rows, rank = kept.shape[2:]
    width = rank // 2
    smem = pl.BlockSpec(memory_space=pltpu.SMEM)
    vmem = pl.BlockSpec(memory_space=pltpu.VMEM)
    away = pl.BlockSpec(memory_space=pl.ANY)
    return pl.pallas_call(
        output_kernel,
        out_shape=(
            jax.ShapeDtypeStruct((rows // lows, 2, lows, width), F32),
            jax.ShapeDtypeStruct((1, rows), F32),
        ),
        in_specs=[smem] + [vmem] * 3 + [away],
        out_specs=(away, vmem),
        scratch_shapes=[
            pltpu.VMEM((rank, table.shape[0]), F32),
            pltpu.VMEM((2, 3, rows, rank), BF16),
            pltpu.VMEM((2, rows // lows, lows, width), F32),
            pltpu.SemaphoreType.DMA((3,)),
        ],
        compiler_params=params(48),
        name="outputs",
    )(where, mine, other, table, kept)


def sketch_table(sketch_perm, rank):
    target = sketch_perm % rank
    sign = 1.0 - 2.0 * (sketch_perm // rank % 2).astype(F32)
    hit = target[:, None] == jnp.arange(rank, dtype=jnp.int32)[None, :]
    return jnp.where(hit, sign[:, None], jnp.zeros((), F32)).astype(BF16)


def swap(value):
    return lax.ppermute(value, "cols", [(0, 1), (1, 0)])


def per_device(factor, gates, gate_layout, jump_masks, jump_rates, sketch_perm, bases, basis_index):
    rows, width = factor.shape
    count = lax.axis_size("wide")
    rank = width * lax.axis_size("cols")
    where = lax.axis_index("cols").astype(jnp.int32).reshape(1)
    gated = apply_gates(gates, gate_layout, factor).reshape(2 * count, -1, width)
    moved = lax.all_to_all(gated, ("wide", "cols"), split_axis=0, concat_axis=0, tiled=True)
    moved = moved.reshape(count, 2, -1, width)
    table = sketch_table(sketch_perm, rank)
    flips = jnp.concatenate([jnp.zeros((1,), jnp.int32), jump_masks])
    coefs = jnp.concatenate([1.0 - 0.5 * jnp.sum(jump_rates, keepdims=True), jnp.sqrt(jump_rates)])
    sketch, keep, send = stack_products(where, flips, coefs, moved, table)
    part = keep + swap(send)
    part, sketch = lax.optimization_barrier((part, sketch))
    total, other = sum_wide(part, swap(sketch))
    turned = rotate_sketch(where, basis_index, sketch, other, bases)
    total, turned = lax.optimization_barrier((total, turned))
    new, weights = outputs(where, total, swap(total), table, turned, moved.shape[2])
    return new.reshape(rows, width), weights


def solution(mesh):
    return jax.shard_map(
        per_device,
        mesh=mesh,
        in_specs=(P("wide", "cols"), P(), P("wide"), P(), P(), P(), P(), P("wide", None)),
        out_specs=(P("wide", "cols"), P("wide", "cols")),
        check_vma=False,
    )
```

```python
import jax
import jax.numpy as jnp
from jax import lax
from jax.experimental import pallas as pl
from jax.experimental.pallas import tpu as pltpu
from jax.sharding import PartitionSpec as P

NS_ITERS = 7
F32 = jnp.float32
BF16 = jnp.bfloat16
NN = (((1,), (0,)), ((), ()))
NT = (((1,), (1,)), ((), ()))


def split(x):
    hi = x.astype(BF16)
    return hi, (x - hi.astype(F32)).astype(BF16)


def dot(a, b, dims=NN):
    return lax.dot_general(a, b, dims, preferred_element_type=F32)


def halves_of(x):
    half = x.shape[0] // 2
    return x[:half], x[half:]


def mul3(a, b, dims=NN):
    left = jnp.concatenate([a[0], a[1], a[0]], axis=dims[0][0][0])
    right = jnp.concatenate([b[0], b[0], b[1]], axis=dims[0][1][0])
    return jnp.concatenate([dot(rows, right, dims) for rows in halves_of(left)], axis=0)


WHOLE = 60


def params(mib):
    return pltpu.CompilerParams(vmem_limit_bytes=int(mib * 2**20))


def gate_kernel(order, layout, gates, factor, out, mats, source, result, sems):
    steps = sems.shape[1] - 1
    chunk = factor.shape[0] // steps
    width = factor.shape[1]
    rows = [pl.ds(i * chunk, chunk) for i in range(steps)]
    first = pltpu.make_async_copy(gates, mats, sems.at[0, steps])
    first.start()
    arrive = []
    leave = []
    for i in range(steps):
        arrive.append(pltpu.make_async_copy(factor.at[rows[i]], source.at[rows[i]], sems.at[0, i]))
        arrive[i].start()
        leave.append(pltpu.make_async_copy(result.at[rows[i]], out.at[rows[i]], sems.at[1, i]))
    first.wait()
    for i in range(steps):
        arrive[i].wait()
        for b in range(i * chunk // order, (i + 1) * chunk // order):
            block = slice(b * order, (b + 1) * order)
            high, low = split(source[block, :])
            left = jnp.concatenate(split(mats[layout[b]]), axis=1)
            right = jnp.concatenate(
                [
                    jnp.concatenate([high, low], axis=1),
                    jnp.concatenate([high, jnp.zeros_like(high)], axis=1),
                ],
                axis=0,
            )
            both = dot(left, right)
            result[block, :] = both[:, :width] + both[:, width:]
        leave[i].start()
    for copy in leave:
        copy.wait()


def apply_gates(gates, layout, factor):
    order = gates.shape[1]
    away = pl.BlockSpec(memory_space=pltpu.HBM)
    steps = 4
    return pl.pallas_call(
        lambda *refs: gate_kernel(order, *refs),
        out_shape=jax.ShapeDtypeStruct(factor.shape, F32),
        in_specs=[pl.BlockSpec(memory_space=pltpu.SMEM), away, away],
        out_specs=away,
        scratch_shapes=[
            pltpu.VMEM(gates.shape, F32),
            pltpu.VMEM(factor.shape, F32),
            pltpu.VMEM(factor.shape, F32),
            pltpu.SemaphoreType.DMA((2, steps + 1)),
        ],
        compiler_params=params(WHOLE),
        name="gates",
    )(layout, gates, factor)


def stack_kernel(where, flips, coefs, moved, table, sketch, keep, send, high, low):
    count, halves, lows, width = moved.shape
    rank = halves * width
    value = [jnp.zeros((count * lows // 2, rank), F32)] * 2
    terms = flips.shape[0]
    for k in range(terms):
        flip = flips[k]
        cols = slice(k * rank, (k + 1) * rank)
        for p in range(count // 2):
            first, second = (2 * p) ^ flip, (2 * p + 1) ^ flip
            rows = slice(p * 2 * lows, (p + 1) * 2 * lows)
            for c in range(halves):
                pair = coefs[k] * jnp.concatenate([moved[first, c], moved[second, c]], axis=0)
                part = slice(k * rank + c * width, k * rank + (c + 1) * width)
                high[rows, part], low[rows, part] = split(pair)
        left = jnp.concatenate([high[:, cols], low[:, cols]], axis=1)
        right = jnp.concatenate([table[cols, :]] * 2, axis=0)
        value = [v + dot(rows, right) for v, rows in zip(value, halves_of(left))]
    value = jnp.concatenate(value, axis=0)
    sketch[...] = value.reshape(sketch.shape)
    left = split(value.T)
    mine = where[0] == 0
    half = rank // 2
    for k in range(terms):
        cols = slice(k * rank, (k + 1) * rank)
        part = mul3(left, (high[:, cols], low[:, cols]))
        for j in range(rank // 128):
            tiles = part[:, j * 128 : (j + 1) * 128]
            top = tiles[:half].reshape(half // 8, 8, 128)
            bottom = tiles[half:].reshape(half // 8, 8, 128)
            keep[:, k * (rank // 128) + j] = jnp.where(mine, top, bottom)
            send[:, k * (rank // 128) + j] = jnp.where(mine, bottom, top)


def stack_products(where, flips, coefs, moved, table):
    count, halves, lows, width = moved.shape
    rank = halves * width
    columns = table.shape[0]
    vmem = pl.BlockSpec(memory_space=pltpu.VMEM)
    smem = pl.BlockSpec(memory_space=pltpu.SMEM)
    half = jax.ShapeDtypeStruct((rank // 16, columns // 128, 8, 128), F32)
    return pl.pallas_call(
        stack_kernel,
        out_shape=(jax.ShapeDtypeStruct((count, lows, rank), F32), half, half),
        in_specs=[smem, smem, smem, vmem, vmem],
        out_specs=(vmem, vmem, vmem),
        scratch_shapes=[pltpu.VMEM((count * lows, columns), BF16)] * 2,
        compiler_params=params(20),
        name="stack",
    )(where, flips, coefs, moved, table)


SIDES = (4, 8, 4)
DEPTH = 2


def groups(count):
    ny, nz, nx = SIDES
    assert ny * nz * nx == count
    at = lambda y, z, x: (y * nz + z) * nx + x
    inside = [(y, d, x) for y in range(ny) for d in range(DEPTH) for x in range(nx)]
    slabs = [[at(y, z + d, x) for y, d, x in inside] for z in range(0, nz, DEPTH)]
    lines = [[at(y, z + d, x) for z in range(0, nz, DEPTH)] for y, d, x in inside]
    return slabs, lines


def spread_kernel(parts, out):
    out[...] = jnp.broadcast_to(jnp.sum(parts[...], axis=0, keepdims=True), out.shape)


def sum_and_spread(parts, copies):
    vmem = pl.BlockSpec(memory_space=pltpu.VMEM)
    return pl.pallas_call(
        spread_kernel,
        out_shape=jax.ShapeDtypeStruct((copies,) + parts.shape[1:], F32),
        in_specs=[vmem],
        out_specs=vmem,
        compiler_params=params(4),
        name="spread",
    )(parts)


def exchange(pieces, members):
    return lax.all_to_all(
        pieces, "wide", split_axis=0, concat_axis=0, axis_index_groups=members, tiled=True
    )


def sum_wide(part, beside):
    slabs, lines = groups(lax.axis_size("wide"))
    members = len(slabs[0])
    tiles = part.shape[0] * part.shape[1] // members
    pieces = exchange(part.reshape((members, tiles) + part.shape[2:]), slabs)
    pieces, beside = lax.optimization_barrier((pieces, beside))
    pieces = exchange(sum_and_spread(pieces, len(lines[0])), lines)
    total = exchange(sum_and_spread(pieces, members), slabs)
    return total.reshape(part.shape), beside


PADDED = 16


def rotate_kernel(
    where, index, own_away, other_away, mats_away, kept,
    own, other, mats, rotated, near, sems,
):
    count, lows, rank = own.shape
    order = mats.shape[1]
    group = order // (2 * lows)
    blocks = rotated.shape[0] // order
    core = where[0]
    mine = core == 0
    arrive = [
        pltpu.make_async_copy(own_away, own, sems.at[0]),
        pltpu.make_async_copy(other_away, other, sems.at[1]),
        pltpu.make_async_copy(mats_away, mats, sems.at[2]),
    ]
    for copy in arrive:
        copy.start()
    for copy in arrive:
        copy.wait()
    for part, value in enumerate(split(own[...].reshape(count * lows, rank))):
        near[part, core] = value
    for part, value in enumerate(split(other[...].reshape(count * lows, rank))):
        near[part, 1 - core] = value
    leave = pltpu.make_async_copy(near.at[:, :2], kept.at[:, :2], sems.at[3])
    leave.start()
    for b in range(blocks):
        parts = []
        for g in range(group):
            w = core * (count // 2) + b * group + g
            first, second = own[w], other[w]
            parts.append(jnp.where(mine, first, second))
            parts.append(jnp.where(mine, second, first))
        data = jnp.concatenate(parts, axis=0)
        value = mul3(split(mats[index[0, core * blocks + b]]), split(data))
        rotated[b * order : (b + 1) * order, :] = value
    for q in range(rotated.shape[0] // rank):
        rows = slice(q * rank, (q + 1) * rank)
        for part, value in enumerate(split(rotated[rows, :].T)):
            near[part, 2, rows] = value
    last = pltpu.make_async_copy(near.at[:, 2], kept.at[:, 2], sems.at[4])
    last.start()
    leave.wait()
    last.wait()


def rotate_sketch(where, index, own, other, bases):
    count, lows, rank = own.shape
    rows = count * lows
    smem = pl.BlockSpec(memory_space=pltpu.SMEM)
    away = pl.BlockSpec(memory_space=pl.ANY)
    return pl.pallas_call(
        rotate_kernel,
        out_shape=jax.ShapeDtypeStruct((2, PADDED, rows, rank), BF16),
        in_specs=[smem, smem, away, away, away],
        out_specs=away,
        scratch_shapes=[
            pltpu.VMEM(own.shape, F32),
            pltpu.VMEM(own.shape, F32),
            pltpu.VMEM(bases.shape, F32),
            pltpu.VMEM((rows, rank), F32),
            pltpu.VMEM((2, 3, rows, rank), BF16),
            pltpu.SemaphoreType.DMA((5,)),
        ],
        compiler_params=params(WHOLE),
        name="rotate",
    )(where, index, own, other, bases)


def frobenius(mat):
    return jnp.sqrt(jnp.sum(jnp.sum(mat * mat, axis=0, keepdims=True), axis=1, keepdims=True))


def eye(n):
    return (
        lax.broadcasted_iota(jnp.int32, (n, n), 0) == lax.broadcasted_iota(jnp.int32, (n, n), 1)
    ).astype(F32)


def newton(mat, value):
    t = mat
    held = None
    for step in range(NS_ITERS):
        last = step == NS_ITERS - 1
        right = split(t)
        if step == 0:
            once = 1.5 * t - 0.5 * mul3(right, right)
            held = 1.5 * eye(t.shape[0]) - 0.5 * t if value is None else once
        else:
            if not last:
                once = 1.5 * t - 0.5 * mul3(right, right)
            held = 1.5 * held - 0.5 * mul3(split(held), right)
        if not last:
            t = 1.5 * once - 0.5 * mul3(split(once), right)
    return held


def output_kernel(where, mine, other, table, away, new, weights, proj, kept, new_near, sems):
    rank = proj.shape[0]
    halves = new.shape[1]
    width = rank // halves
    fetch = pltpu.make_async_copy(away.at[:, : kept.shape[1]], kept, sems.at[2])
    fetch.start()
    first = pl.ds(pl.multiple_of(where[0] * width, width), width)
    second = pl.ds(pl.multiple_of((1 - where[0]) * width, width), width)
    for j in range(mine.shape[1]):
        cols = slice(j * 128, (j + 1) * 128)
        proj[first, cols] = mine[:, j].reshape(width, 128)
        proj[second, cols] = other[:, j].reshape(width, 128)
    p = split(proj[...])
    left = jnp.concatenate(p, axis=1)
    right = jnp.concatenate([table[...]] * 2, axis=0)
    gram = jnp.concatenate([dot(part, right) for part in halves_of(left)], axis=0)
    inverse = newton(gram / (frobenius(gram) + 1e-6), None)
    inv = split(inverse)
    coeff = split(mul3(inv, p))
    core = mul3(coeff, coeff, NT)
    shift = frobenius(core) + 1e-6
    root = split(newton(core / shift, "approx"))
    scale = jnp.sqrt(shift)
    mixing = scale * mul3(inv, root)
    turned = split(scale * mul3(root, inv))
    high, low = split(jnp.where(where[0] == 0, mixing[:, :width], mixing[:, width:]))
    right = jnp.concatenate(
        [
            jnp.concatenate([high, low], axis=1),
            jnp.concatenate([high, jnp.zeros_like(high)], axis=1),
        ],
        axis=0,
    )
    fetch.wait()
    leave = []
    for c in range(halves):
        left = jnp.concatenate([kept[0, c], kept[1, c]], axis=1)
        both = jnp.concatenate([dot(part, right) for part in halves_of(left)], axis=0)
        value = both[:, :width] + both[:, width:]
        new_near[c] = value.reshape(new_near.shape[1:])
        leave.append(pltpu.make_async_copy(new_near.at[c], new.at[:, c], sems.at[c]))
        leave[c].start()
    for q in range(kept.shape[2] // rank):
        rows = slice(q * rank, (q + 1) * rank)
        turn = mul3(turned, (kept[0, 2, rows], kept[1, 2, rows]))
        weights[:, rows] = jnp.sum(turn * turn, axis=0, keepdims=True) / rank
    for copy in leave:
        copy.wait()


def outputs(where, mine, other, table, kept, lows):
    rows, rank = kept.shape[2:]
    width = rank // 2
    smem = pl.BlockSpec(memory_space=pltpu.SMEM)
    vmem = pl.BlockSpec(memory_space=pltpu.VMEM)
    away = pl.BlockSpec(memory_space=pl.ANY)
    return pl.pallas_call(
        output_kernel,
        out_shape=(
            jax.ShapeDtypeStruct((rows // lows, 2, lows, width), F32),
            jax.ShapeDtypeStruct((1, rows), F32),
        ),
        in_specs=[smem] + [vmem] * 3 + [away],
        out_specs=(away, vmem),
        scratch_shapes=[
            pltpu.VMEM((rank, table.shape[0]), F32),
            pltpu.VMEM((2, 3, rows, rank), BF16),
            pltpu.VMEM((2, rows // lows, lows, width), F32),
            pltpu.SemaphoreType.DMA((3,)),
        ],
        compiler_params=params(48),
        name="outputs",
    )(where, mine, other, table, kept)


def sketch_table(sketch_perm, rank):
    target = sketch_perm % rank
    sign = 1.0 - 2.0 * (sketch_perm // rank % 2).astype(F32)
    hit = target[:, None] == jnp.arange(rank, dtype=jnp.int32)[None, :]
    return jnp.where(hit, sign[:, None], jnp.zeros((), F32)).astype(BF16)


def swap(value):
    return lax.ppermute(value, "cols", [(0, 1), (1, 0)])


def per_device(factor, gates, gate_layout, jump_masks, jump_rates, sketch_perm, bases, basis_index):
    rows, width = factor.shape
    count = lax.axis_size("wide")
    rank = width * lax.axis_size("cols")
    where = lax.axis_index("cols").astype(jnp.int32).reshape(1)
    gated = apply_gates(gates, gate_layout, factor).reshape(2 * count, -1, width)
    moved = lax.all_to_all(gated, ("wide", "cols"), split_axis=0, concat_axis=0, tiled=True)
    moved = moved.reshape(count, 2, -1, width)
    table = sketch_table(sketch_perm, rank)
    flips = jnp.concatenate([jnp.zeros((1,), jnp.int32), jump_masks])
    coefs = jnp.concatenate([1.0 - 0.5 * jnp.sum(jump_rates, keepdims=True), jnp.sqrt(jump_rates)])
    sketch, keep, send = stack_products(where, flips, coefs, moved, table)
    part = keep + swap(send)
    part, sketch = lax.optimization_barrier((part, sketch))
    total, other = sum_wide(part, swap(sketch))
    turned = rotate_sketch(where, basis_index, sketch, other, bases)
    total, turned = lax.optimization_barrier((total, turned))
    new, weights = outputs(where, total, swap(total), table, turned, moved.shape[2])
    return new.reshape(rows, width), weights


def solution(mesh):
    return jax.shard_map(
        per_device,
        mesh=mesh,
        in_specs=(P("wide", "cols"), P(), P("wide"), P(), P(), P(), P(), P("wide", None)),
        out_specs=(P("wide", "cols"), P("wide", "cols")),
        check_vma=False,
    )
```

```python
import jax
import jax.numpy as jnp
from jax import lax
from jax.experimental import pallas as pl
from jax.experimental.pallas import tpu as pltpu
from jax.sharding import PartitionSpec as P

NS_ITERS = 7
F32 = jnp.float32
BF16 = jnp.bfloat16
NN = (((1,), (0,)), ((), ()))
NT = (((1,), (1,)), ((), ()))


def split(x):
    hi = x.astype(BF16)
    return hi, (x - hi.astype(F32)).astype(BF16)


def dot(a, b, dims=NN):
    return lax.dot_general(a, b, dims, preferred_element_type=F32)


def halves_of(x):
    half = x.shape[0] // 2
    return x[:half], x[half:]


def joined(a, b, dims=NN):
    left = jnp.concatenate([a[0], a[1], a[0]], axis=dims[0][0][0])
    right = jnp.concatenate([b[0], b[0], b[1]], axis=dims[0][1][0])
    return left, right


def mul3(a, b, dims=NN):
    return dot(*joined(a, b, dims), dims)


def mul3_rows(a, b):
    left, right = joined(a, b)
    return jnp.concatenate([dot(rows, right) for rows in halves_of(left)], axis=0)


def blocks_of(a, size):
    cuts = range(0, a[0].shape[1], size)
    return [tuple(part[:, i : i + size] for part in a) for i in cuts]


WHOLE = 60


def params(mib):
    return pltpu.CompilerParams(vmem_limit_bytes=int(mib * 2**20))


def gate_kernel(order, layout, gates, factor, out, mats, source, result, sems):
    steps = sems.shape[1] - 1
    chunk = factor.shape[0] // steps
    width = factor.shape[1]
    rows = [pl.ds(i * chunk, chunk) for i in range(steps)]
    first = pltpu.make_async_copy(gates, mats, sems.at[0, steps])
    first.start()
    arrive = []
    leave = []
    for i in range(steps):
        arrive.append(pltpu.make_async_copy(factor.at[rows[i]], source.at[rows[i]], sems.at[0, i]))
        arrive[i].start()
        leave.append(pltpu.make_async_copy(result.at[rows[i]], out.at[rows[i]], sems.at[1, i]))
    first.wait()
    for i in range(steps):
        arrive[i].wait()
        for b in range(i * chunk // order, (i + 1) * chunk // order):
            block = slice(b * order, (b + 1) * order)
            high, low = split(source[block, :])
            left = jnp.concatenate(split(mats[layout[b]]), axis=1)
            right = jnp.concatenate(
                [
                    jnp.concatenate([high, low], axis=1),
                    jnp.concatenate([high, jnp.zeros_like(high)], axis=1),
                ],
                axis=0,
            )
            both = dot(left, right)
            result[block, :] = both[:, :width] + both[:, width:]
        leave[i].start()
    for copy in leave:
        copy.wait()


def apply_gates(gates, layout, factor):
    order = gates.shape[1]
    away = pl.BlockSpec(memory_space=pltpu.HBM)
    steps = 4
    return pl.pallas_call(
        lambda *refs: gate_kernel(order, *refs),
        out_shape=jax.ShapeDtypeStruct(factor.shape, F32),
        in_specs=[pl.BlockSpec(memory_space=pltpu.SMEM), away, away],
        out_specs=away,
        scratch_shapes=[
            pltpu.VMEM(gates.shape, F32),
            pltpu.VMEM(factor.shape, F32),
            pltpu.VMEM(factor.shape, F32),
            pltpu.SemaphoreType.DMA((2, steps + 1)),
        ],
        compiler_params=params(WHOLE),
        name="gates",
    )(layout, gates, factor)


def stack_kernel(where, flips, coefs, moved, table, sketch, keep, send, high, low):
    count, halves, lows, width = moved.shape
    rank = halves * width
    value = [jnp.zeros((count * lows // 2, rank), F32)] * 2
    terms = flips.shape[0]
    for k in range(terms):
        flip = flips[k]
        cols = slice(k * rank, (k + 1) * rank)
        for p in range(count // 2):
            first, second = (2 * p) ^ flip, (2 * p + 1) ^ flip
            rows = slice(p * 2 * lows, (p + 1) * 2 * lows)
            for c in range(halves):
                pair = coefs[k] * jnp.concatenate([moved[first, c], moved[second, c]], axis=0)
                part = slice(k * rank + c * width, k * rank + (c + 1) * width)
                high[rows, part], low[rows, part] = split(pair)
        left = jnp.concatenate([high[:, cols], low[:, cols]], axis=1)
        right = jnp.concatenate([table[cols, :]] * 2, axis=0)
        value = [v + dot(rows, right) for v, rows in zip(value, halves_of(left))]
    value = jnp.concatenate(value, axis=0)
    sketch[...] = value.reshape(sketch.shape)
    left = split(value.T)
    mine = where[0] == 0
    half = rank // 2
    for k in range(terms):
        cols = slice(k * rank, (k + 1) * rank)
        part = mul3(left, (high[:, cols], low[:, cols]))
        for j in range(rank // 128):
            tiles = part[:, j * 128 : (j + 1) * 128]
            top = tiles[:half].reshape(half // 8, 8, 128)
            bottom = tiles[half:].reshape(half // 8, 8, 128)
            keep[:, k * (rank // 128) + j] = jnp.where(mine, top, bottom)
            send[:, k * (rank // 128) + j] = jnp.where(mine, bottom, top)


def stack_products(where, flips, coefs, moved, table):
    count, halves, lows, width = moved.shape
    rank = halves * width
    columns = table.shape[0]
    vmem = pl.BlockSpec(memory_space=pltpu.VMEM)
    smem = pl.BlockSpec(memory_space=pltpu.SMEM)
    half = jax.ShapeDtypeStruct((rank // 16, columns // 128, 8, 128), F32)
    return pl.pallas_call(
        stack_kernel,
        out_shape=(jax.ShapeDtypeStruct((count, lows, rank), F32), half, half),
        in_specs=[smem, smem, smem, vmem, vmem],
        out_specs=(vmem, vmem, vmem),
        scratch_shapes=[pltpu.VMEM((count * lows, columns), BF16)] * 2,
        compiler_params=params(20),
        name="stack",
    )(where, flips, coefs, moved, table)


SIDES = (4, 8, 4)
DEPTH = 2


def groups(count):
    ny, nz, nx = SIDES
    assert ny * nz * nx == count
    at = lambda y, z, x: (y * nz + z) * nx + x
    inside = [(y, d, x) for y in range(ny) for d in range(DEPTH) for x in range(nx)]
    slabs = [[at(y, z + d, x) for y, d, x in inside] for z in range(0, nz, DEPTH)]
    lines = [[at(y, z + d, x) for z in range(0, nz, DEPTH)] for y, d, x in inside]
    return slabs, lines


def sum_kernel(parts, out):
    out[...] = jnp.sum(parts[...], axis=0)


def spread_kernel(*refs):
    total = refs[0][...]
    for part in refs[1:-1]:
        total = total + part[...]
    refs[-1][...] = jnp.broadcast_to(total[None], refs[-1].shape)


def local(kernel, shape, name, *args):
    vmem = pl.BlockSpec(memory_space=pltpu.VMEM)
    return pl.pallas_call(
        kernel,
        out_shape=jax.ShapeDtypeStruct(shape, F32),
        in_specs=[vmem] * len(args),
        out_specs=vmem,
        compiler_params=params(4),
        name=name,
    )(*args)


def exchange(pieces, members):
    return lax.all_to_all(
        pieces, "wide", split_axis=0, concat_axis=0, axis_index_groups=members, tiled=True
    )


def sum_wide(part, beside):
    slabs, lines = groups(lax.axis_size("wide"))
    members = len(slabs[0])
    tiles = part.shape[0] * part.shape[1] // members
    pieces = exchange(part.reshape((members, tiles) + part.shape[2:]), slabs)
    pieces, beside = lax.optimization_barrier((pieces, beside))
    mine = local(sum_kernel, pieces.shape[1:], "sum", pieces)
    terms = [mine]
    for step in range(1, len(lines[0])):
        pairs = [(at, line[(i + step) % len(line)]) for line in lines for i, at in enumerate(line)]
        terms.append(lax.ppermute(mine, "wide", pairs))
    copies = local(spread_kernel, pieces.shape, "spread", *terms)
    total = exchange(copies, slabs)
    return total.reshape(part.shape), beside


PADDED = 16


def rotate_kernel(
    where, index, own_away, other_away, mats_away, kept,
    own, other, mats, rotated, near, sems,
):
    count, lows, rank = own.shape
    order = mats.shape[1]
    group = order // (2 * lows)
    blocks = rotated.shape[0] // order
    core = where[0]
    mine = core == 0
    arrive = [
        pltpu.make_async_copy(own_away, own, sems.at[0]),
        pltpu.make_async_copy(other_away, other, sems.at[1]),
        pltpu.make_async_copy(mats_away, mats, sems.at[2]),
    ]
    for copy in arrive:
        copy.start()
    for copy in arrive:
        copy.wait()
    for part, value in enumerate(split(own[...].reshape(count * lows, rank))):
        near[part, core] = value
    for part, value in enumerate(split(other[...].reshape(count * lows, rank))):
        near[part, 1 - core] = value
    leave = pltpu.make_async_copy(near.at[:, :2], kept.at[:, :2], sems.at[3])
    leave.start()
    for b in range(blocks):
        parts = []
        for g in range(group):
            w = core * (count // 2) + b * group + g
            first, second = own[w], other[w]
            parts.append(jnp.where(mine, first, second))
            parts.append(jnp.where(mine, second, first))
        data = jnp.concatenate(parts, axis=0)
        value = mul3_rows(split(mats[index[0, core * blocks + b]]), split(data))
        rotated[b * order : (b + 1) * order, :] = value
    for q in range(rotated.shape[0] // rank):
        rows = slice(q * rank, (q + 1) * rank)
        for part, value in enumerate(split(rotated[rows, :].T)):
            near[part, 2, rows] = value
    last = pltpu.make_async_copy(near.at[:, 2], kept.at[:, 2], sems.at[4])
    last.start()
    leave.wait()
    last.wait()


def rotate_sketch(where, index, own, other, bases):
    count, lows, rank = own.shape
    rows = count * lows
    smem = pl.BlockSpec(memory_space=pltpu.SMEM)
    away = pl.BlockSpec(memory_space=pl.ANY)
    return pl.pallas_call(
        rotate_kernel,
        out_shape=jax.ShapeDtypeStruct((2, PADDED, rows, rank), BF16),
        in_specs=[smem, smem, away, away, away],
        out_specs=away,
        scratch_shapes=[
            pltpu.VMEM(own.shape, F32),
            pltpu.VMEM(own.shape, F32),
            pltpu.VMEM(bases.shape, F32),
            pltpu.VMEM((rows, rank), F32),
            pltpu.VMEM((2, 3, rows, rank), BF16),
            pltpu.SemaphoreType.DMA((5,)),
        ],
        compiler_params=params(WHOLE),
        name="rotate",
    )(where, index, own, other, bases)


def frobenius(mat):
    return jnp.sqrt(jnp.sum(jnp.sum(mat * mat, axis=0, keepdims=True), axis=1, keepdims=True))


def eye(n):
    return (
        lax.broadcasted_iota(jnp.int32, (n, n), 0) == lax.broadcasted_iota(jnp.int32, (n, n), 1)
    ).astype(F32)


def newton(mat, value):
    t = mat
    held = None
    for step in range(NS_ITERS):
        last = step == NS_ITERS - 1
        right = split(t)
        if step == 0:
            once = 1.5 * t - 0.5 * mul3_rows(right, right)
            held = 1.5 * eye(t.shape[0]) - 0.5 * t if value is None else once
        else:
            if not last:
                once = 1.5 * t - 0.5 * mul3_rows(right, right)
            held = 1.5 * held - 0.5 * mul3_rows(split(held), right)
        if not last:
            t = 1.5 * once - 0.5 * mul3_rows(split(once), right)
    return held


def output_kernel(where, mine, other, table, away, new, weights, proj, kept, new_near, sems):
    rank = proj.shape[0]
    halves = new.shape[1]
    width = rank // halves
    fetch = pltpu.make_async_copy(away.at[:, : kept.shape[1]], kept, sems.at[2])
    fetch.start()
    first = pl.ds(pl.multiple_of(where[0] * width, width), width)
    second = pl.ds(pl.multiple_of((1 - where[0]) * width, width), width)
    for j in range(mine.shape[1]):
        cols = slice(j * 128, (j + 1) * 128)
        proj[first, cols] = mine[:, j].reshape(width, 128)
        proj[second, cols] = other[:, j].reshape(width, 128)
    p = split(proj[...])
    gram = 0.0
    for k, part in enumerate(blocks_of(p, rank)):
        signs = table[k * rank : (k + 1) * rank]
        left = jnp.concatenate(part, axis=1)
        gram = gram + dot(left, jnp.concatenate([signs] * 2, axis=0))
    inverse = newton(gram / (frobenius(gram) + 1e-6), None)
    inv = split(inverse)
    core = 0.0
    for part in blocks_of(p, rank):
        coeff = split(mul3(inv, part))
        core = core + mul3(coeff, coeff, NT)
    shift = frobenius(core) + 1e-6
    root = split(newton(core / shift, "approx"))
    scale = jnp.sqrt(shift)
    mixing = scale * mul3(inv, root)
    turned = split(scale * mul3(root, inv))
    high, low = split(jnp.where(where[0] == 0, mixing[:, :width], mixing[:, width:]))
    right = jnp.concatenate(
        [
            jnp.concatenate([high, low], axis=1),
            jnp.concatenate([high, jnp.zeros_like(high)], axis=1),
        ],
        axis=0,
    )
    fetch.wait()
    leave = []
    for c in range(halves):
        left = jnp.concatenate([kept[0, c], kept[1, c]], axis=1)
        both = jnp.concatenate([dot(part, right) for part in halves_of(left)], axis=0)
        value = both[:, :width] + both[:, width:]
        new_near[c] = value.reshape(new_near.shape[1:])
        leave.append(pltpu.make_async_copy(new_near.at[c], new.at[:, c], sems.at[c]))
        leave[c].start()
    for q in range(kept.shape[2] // rank):
        rows = slice(q * rank, (q + 1) * rank)
        turn = mul3(turned, (kept[0, 2, rows], kept[1, 2, rows]))
        weights[:, rows] = jnp.sum(turn * turn, axis=0, keepdims=True) / rank
    for copy in leave:
        copy.wait()


def outputs(where, mine, other, table, kept, lows):
    rows, rank = kept.shape[2:]
    width = rank // 2
    smem = pl.BlockSpec(memory_space=pltpu.SMEM)
    vmem = pl.BlockSpec(memory_space=pltpu.VMEM)
    away = pl.BlockSpec(memory_space=pl.ANY)
    return pl.pallas_call(
        output_kernel,
        out_shape=(
            jax.ShapeDtypeStruct((rows // lows, 2, lows, width), F32),
            jax.ShapeDtypeStruct((1, rows), F32),
        ),
        in_specs=[smem] + [vmem] * 3 + [away],
        out_specs=(away, vmem),
        scratch_shapes=[
            pltpu.VMEM((rank, table.shape[0]), F32),
            pltpu.VMEM((2, 3, rows, rank), BF16),
            pltpu.VMEM((2, rows // lows, lows, width), F32),
            pltpu.SemaphoreType.DMA((3,)),
        ],
        compiler_params=params(48),
        name="outputs",
    )(where, mine, other, table, kept)


def sketch_table(sketch_perm, rank):
    target = sketch_perm % rank
    sign = 1.0 - 2.0 * (sketch_perm // rank % 2).astype(F32)
    hit = target[:, None] == jnp.arange(rank, dtype=jnp.int32)[None, :]
    return jnp.where(hit, sign[:, None], jnp.zeros((), F32)).astype(BF16)


def swap(value):
    return lax.ppermute(value, "cols", [(0, 1), (1, 0)])


def per_device(factor, gates, gate_layout, jump_masks, jump_rates, sketch_perm, bases, basis_index):
    rows, width = factor.shape
    count = lax.axis_size("wide")
    rank = width * lax.axis_size("cols")
    where = lax.axis_index("cols").astype(jnp.int32).reshape(1)
    gated = apply_gates(gates, gate_layout, factor).reshape(2 * count, -1, width)
    moved = lax.all_to_all(gated, ("wide", "cols"), split_axis=0, concat_axis=0, tiled=True)
    moved = moved.reshape(count, 2, -1, width)
    table = sketch_table(sketch_perm, rank)
    flips = jnp.concatenate([jnp.zeros((1,), jnp.int32), jump_masks])
    coefs = jnp.concatenate([1.0 - 0.5 * jnp.sum(jump_rates, keepdims=True), jnp.sqrt(jump_rates)])
    sketch, keep, send = stack_products(where, flips, coefs, moved, table)
    part = keep + swap(send)
    part, sketch = lax.optimization_barrier((part, sketch))
    total, other = sum_wide(part, swap(sketch))
    turned = rotate_sketch(where, basis_index, sketch, other, bases)
    total, turned = lax.optimization_barrier((total, turned))
    new, weights = outputs(where, total, swap(total), table, turned, moved.shape[2])
    return new.reshape(rows, width), weights


def solution(mesh):
    return jax.shard_map(
        per_device,
        mesh=mesh,
        in_specs=(P("wide", "cols"), P(), P("wide"), P(), P(), P(), P(), P("wide", None)),
        out_specs=(P("wide", "cols"), P("wide", "cols")),
        check_vma=False,
    )
```

```python
import jax
import jax.numpy as jnp
from jax import lax
from jax.experimental import pallas as pl
from jax.experimental.pallas import tpu as pltpu
from jax.sharding import PartitionSpec as P

NS_ITERS = 7
F32 = jnp.float32
BF16 = jnp.bfloat16
NN = (((1,), (0,)), ((), ()))
NT = (((1,), (1,)), ((), ()))


def split(x):
    hi = x.astype(BF16)
    return hi, (x - hi.astype(F32)).astype(BF16)


def dot(a, b, dims=NN):
    return lax.dot_general(a, b, dims, preferred_element_type=F32)


def halves_of(x):
    half = x.shape[0] // 2
    return x[:half], x[half:]


def joined(a, b, dims=NN):
    left = jnp.concatenate([a[0], a[1], a[0]], axis=dims[0][0][0])
    right = jnp.concatenate([b[0], b[0], b[1]], axis=dims[0][1][0])
    return left, right


def mul3(a, b, dims=NN):
    return dot(*joined(a, b, dims), dims)


def mul3_rows(a, b):
    left, right = joined(a, b)
    return jnp.concatenate([dot(rows, right) for rows in halves_of(left)], axis=0)


def blocks_of(a, size):
    cuts = range(0, a[0].shape[1], size)
    return [tuple(part[:, i : i + size] for part in a) for i in cuts]


WHOLE = 60


def params(mib):
    return pltpu.CompilerParams(vmem_limit_bytes=int(mib * 2**20))


def gate_kernel(order, layout, gates, factor, out, mats, source, result, sems):
    steps = sems.shape[1] - 1
    chunk = factor.shape[0] // steps
    width = factor.shape[1]
    rows = [pl.ds(i * chunk, chunk) for i in range(steps)]
    first = pltpu.make_async_copy(gates, mats, sems.at[0, steps])
    first.start()
    arrive = []
    leave = []
    for i in range(steps):
        arrive.append(pltpu.make_async_copy(factor.at[rows[i]], source.at[rows[i]], sems.at[0, i]))
        arrive[i].start()
        leave.append(pltpu.make_async_copy(result.at[rows[i]], out.at[rows[i]], sems.at[1, i]))
    first.wait()
    for i in range(steps):
        arrive[i].wait()
        for b in range(i * chunk // order, (i + 1) * chunk // order):
            block = slice(b * order, (b + 1) * order)
            high, low = split(source[block, :])
            left = jnp.concatenate(split(mats[layout[b]]), axis=1)
            right = jnp.concatenate(
                [
                    jnp.concatenate([high, low], axis=1),
                    jnp.concatenate([high, jnp.zeros_like(high)], axis=1),
                ],
                axis=0,
            )
            both = dot(left, right)
            result[block, :] = both[:, :width] + both[:, width:]
        leave[i].start()
    for copy in leave:
        copy.wait()


def apply_gates(gates, layout, factor):
    order = gates.shape[1]
    away = pl.BlockSpec(memory_space=pltpu.HBM)
    steps = 2
    return pl.pallas_call(
        lambda *refs: gate_kernel(order, *refs),
        out_shape=jax.ShapeDtypeStruct(factor.shape, F32),
        in_specs=[pl.BlockSpec(memory_space=pltpu.SMEM), away, away],
        out_specs=away,
        scratch_shapes=[
            pltpu.VMEM(gates.shape, F32),
            pltpu.VMEM(factor.shape, F32),
            pltpu.VMEM(factor.shape, F32),
            pltpu.SemaphoreType.DMA((2, steps + 1)),
        ],
        compiler_params=params(WHOLE),
        name="gates",
    )(layout, gates, factor)


def stack_kernel(where, flips, coefs, moved, table, sketch, keep, send, high, low):
    count, halves, lows, width = moved.shape
    rank = halves * width
    value = [jnp.zeros((count * lows // 2, rank), F32)] * 2
    terms = flips.shape[0]
    for k in range(terms):
        flip = flips[k]
        cols = slice(k * rank, (k + 1) * rank)
        for p in range(count // 2):
            first, second = (2 * p) ^ flip, (2 * p + 1) ^ flip
            rows = slice(p * 2 * lows, (p + 1) * 2 * lows)
            for c in range(halves):
                pair = coefs[k] * jnp.concatenate([moved[first, c], moved[second, c]], axis=0)
                part = slice(k * rank + c * width, k * rank + (c + 1) * width)
                high[rows, part], low[rows, part] = split(pair)
        left = jnp.concatenate([high[:, cols], low[:, cols]], axis=1)
        right = jnp.concatenate([table[cols, :]] * 2, axis=0)
        value = [v + dot(rows, right) for v, rows in zip(value, halves_of(left))]
    value = jnp.concatenate(value, axis=0)
    sketch[...] = value.reshape(sketch.shape)
    left = split(value.T)
    mine = where[0] == 0
    half = rank // 2
    for k in range(terms):
        cols = slice(k * rank, (k + 1) * rank)
        part = mul3(left, (high[:, cols], low[:, cols]))
        for j in range(rank // 128):
            tiles = part[:, j * 128 : (j + 1) * 128]
            top = tiles[:half].reshape(half // 8, 8, 128)
            bottom = tiles[half:].reshape(half // 8, 8, 128)
            keep[:, k * (rank // 128) + j] = jnp.where(mine, top, bottom)
            send[:, k * (rank // 128) + j] = jnp.where(mine, bottom, top)


def stack_products(where, flips, coefs, moved, table):
    count, halves, lows, width = moved.shape
    rank = halves * width
    columns = table.shape[0]
    vmem = pl.BlockSpec(memory_space=pltpu.VMEM)
    smem = pl.BlockSpec(memory_space=pltpu.SMEM)
    half = jax.ShapeDtypeStruct((rank // 16, columns // 128, 8, 128), F32)
    return pl.pallas_call(
        stack_kernel,
        out_shape=(jax.ShapeDtypeStruct((count, lows, rank), F32), half, half),
        in_specs=[smem, smem, smem, vmem, vmem],
        out_specs=(vmem, vmem, vmem),
        scratch_shapes=[pltpu.VMEM((count * lows, columns), BF16)] * 2,
        compiler_params=params(20),
        name="stack",
    )(where, flips, coefs, moved, table)


SIDES = (4, 8, 4)
DEPTH = 2


def groups(count):
    ny, nz, nx = SIDES
    assert ny * nz * nx == count
    at = lambda y, z, x: (y * nz + z) * nx + x
    inside = [(y, d, x) for y in range(ny) for d in range(DEPTH) for x in range(nx)]
    slabs = [[at(y, z + d, x) for y, d, x in inside] for z in range(0, nz, DEPTH)]
    lines = [[at(y, z + d, x) for z in range(0, nz, DEPTH)] for y, d, x in inside]
    return slabs, lines


def spread_kernel(parts, out):
    out[...] = jnp.broadcast_to(jnp.sum(parts[...], axis=0, keepdims=True), out.shape)


def sum_and_spread(parts, copies):
    vmem = pl.BlockSpec(memory_space=pltpu.VMEM)
    return pl.pallas_call(
        spread_kernel,
        out_shape=jax.ShapeDtypeStruct((copies,) + parts.shape[1:], F32),
        in_specs=[vmem],
        out_specs=vmem,
        compiler_params=params(4),
        name="spread",
    )(parts)


def exchange(pieces, members):
    return lax.all_to_all(
        pieces, "wide", split_axis=0, concat_axis=0, axis_index_groups=members, tiled=True
    )


def sum_wide(part, beside):
    slabs, lines = groups(lax.axis_size("wide"))
    members = len(slabs[0])
    tiles = part.shape[0] * part.shape[1] // members
    pieces = exchange(part.reshape((members, tiles) + part.shape[2:]), slabs)
    pieces, beside = lax.optimization_barrier((pieces, beside))
    pieces = exchange(sum_and_spread(pieces, len(lines[0])), lines)
    total = exchange(sum_and_spread(pieces, members), slabs)
    return total.reshape(part.shape), beside


PADDED = 16


def rotate_kernel(where, index, own, other, mats_away, kept, rows, mats, rotated, turned, sems):
    count, lows, rank = own.shape
    order = mats.shape[1]
    group = order // (2 * lows)
    blocks = rotated.shape[0] // order
    core = where[0]
    near = [
        pltpu.make_async_copy(own, rows.at[core], sems.at[0]),
        pltpu.make_async_copy(other, rows.at[1 - core], sems.at[1]),
        pltpu.make_async_copy(mats_away, mats, sems.at[2]),
    ]
    through = [pltpu.make_async_copy(rows, kept.at[:2], sems.at[3])]
    for copy in near:
        copy.start()
    for copy in near:
        copy.wait()
    through[0].start()
    for b in range(blocks):
        parts = []
        for g in range(group):
            w = core * (count // 2) + b * group + g
            parts += [rows[0, w], rows[1, w]]
        data = jnp.concatenate(parts, axis=0)
        value = mul3_rows(split(mats[index[0, core * blocks + b]]), split(data))
        rotated[b * order : (b + 1) * order, :] = value
    for q in range(rotated.shape[0] // rank):
        cut = slice(q * rank, (q + 1) * rank)
        tile = rotated[cut, :].T
        turned[q * rank // lows : (q + 1) * rank // lows] = tile.reshape(-1, lows, rank)
    last = pltpu.make_async_copy(turned, kept.at[2], sems.at[4])
    last.start()
    for copy in through + [last]:
        copy.wait()


def rotate_sketch(where, index, own, other, bases):
    count, lows, rank = own.shape
    smem = pl.BlockSpec(memory_space=pltpu.SMEM)
    away = pl.BlockSpec(memory_space=pl.ANY)
    return pl.pallas_call(
        rotate_kernel,
        out_shape=jax.ShapeDtypeStruct((PADDED,) + own.shape, F32),
        in_specs=[smem, smem, away, away, away],
        out_specs=away,
        scratch_shapes=[
            pltpu.VMEM((2, count, lows, rank), F32),
            pltpu.VMEM(bases.shape, F32),
            pltpu.VMEM((count * lows, rank), F32),
            pltpu.VMEM(own.shape, F32),
            pltpu.SemaphoreType.DMA((5,)),
        ],
        compiler_params=params(WHOLE),
        name="rotate",
    )(where, index, own, other, bases)


def frobenius(mat):
    return jnp.sqrt(jnp.sum(jnp.sum(mat * mat, axis=0, keepdims=True), axis=1, keepdims=True))


def eye(n):
    return (
        lax.broadcasted_iota(jnp.int32, (n, n), 0) == lax.broadcasted_iota(jnp.int32, (n, n), 1)
    ).astype(F32)


def newton(mat, value):
    t = mat
    held = None
    for step in range(NS_ITERS):
        last = step == NS_ITERS - 1
        right = split(t)
        if step == 0:
            once = 1.5 * t - 0.5 * mul3_rows(right, right)
            held = 1.5 * eye(t.shape[0]) - 0.5 * t if value is None else once
        else:
            if not last:
                once = 1.5 * t - 0.5 * mul3_rows(right, right)
            held = 1.5 * held - 0.5 * mul3_rows(split(held), right)
        if not last:
            t = 1.5 * once - 0.5 * mul3_rows(split(once), right)
    return held


def output_kernel(where, mine, other, table, away, new, weights, proj, near, kept, new_near, sems):
    rank = proj.shape[0]
    halves = new.shape[1]
    width = rank // halves
    fetch = pltpu.make_async_copy(away.at[: near.shape[0]], near, sems.at[2])
    fetch.start()
    first = pl.ds(pl.multiple_of(where[0] * width, width), width)
    second = pl.ds(pl.multiple_of((1 - where[0]) * width, width), width)
    for j in range(mine.shape[1]):
        cols = slice(j * 128, (j + 1) * 128)
        proj[first, cols] = mine[:, j].reshape(width, 128)
        proj[second, cols] = other[:, j].reshape(width, 128)
    p = split(proj[...])
    gram = 0.0
    for k, part in enumerate(blocks_of(p, rank)):
        signs = table[k * rank : (k + 1) * rank]
        left = jnp.concatenate(part, axis=1)
        gram = gram + dot(left, jnp.concatenate([signs] * 2, axis=0))
    inverse = newton(gram / (frobenius(gram) + 1e-6), None)
    inv = split(inverse)
    core = 0.0
    for part in blocks_of(p, rank):
        coeff = split(mul3(inv, part))
        core = core + mul3(coeff, coeff, NT)
    fetch.wait()
    for i in range(near.shape[0]):
        kept[0, i], kept[1, i] = split(near[i].reshape(kept.shape[2:]))
    shift = frobenius(core) + 1e-6
    root = split(newton(core / shift, "approx"))
    scale = jnp.sqrt(shift)
    mixing = scale * mul3(inv, root)
    turned = split(scale * mul3(root, inv))
    high, low = split(jnp.where(where[0] == 0, mixing[:, :width], mixing[:, width:]))
    right = jnp.concatenate(
        [
            jnp.concatenate([high, low], axis=1),
            jnp.concatenate([high, jnp.zeros_like(high)], axis=1),
        ],
        axis=0,
    )
    leave = []
    for c in range(halves):
        left = jnp.concatenate([kept[0, c], kept[1, c]], axis=1)
        both = jnp.concatenate([dot(part, right) for part in halves_of(left)], axis=0)
        value = both[:, :width] + both[:, width:]
        new_near[c] = value.reshape(new_near.shape[1:])
        leave.append(pltpu.make_async_copy(new_near.at[c], new.at[:, c], sems.at[c]))
        leave[c].start()
    for q in range(kept.shape[2] // rank):
        rows = slice(q * rank, (q + 1) * rank)
        turn = mul3(turned, (kept[0, 2, rows], kept[1, 2, rows]))
        weights[:, rows] = jnp.sum(turn * turn, axis=0, keepdims=True) / rank
    for copy in leave:
        copy.wait()


def outputs(where, mine, other, table, kept):
    count, lows, rank = kept.shape[1:]
    rows = count * lows
    width = rank // 2
    smem = pl.BlockSpec(memory_space=pltpu.SMEM)
    vmem = pl.BlockSpec(memory_space=pltpu.VMEM)
    away = pl.BlockSpec(memory_space=pl.ANY)
    return pl.pallas_call(
        output_kernel,
        out_shape=(
            jax.ShapeDtypeStruct((rows // lows, 2, lows, width), F32),
            jax.ShapeDtypeStruct((1, rows), F32),
        ),
        in_specs=[smem] + [vmem] * 3 + [away],
        out_specs=(away, vmem),
        scratch_shapes=[
            pltpu.VMEM((rank, table.shape[0]), F32),
            pltpu.VMEM((3, count, lows, rank), F32),
            pltpu.VMEM((2, 3, rows, rank), BF16),
            pltpu.VMEM((2, rows // lows, lows, width), F32),
            pltpu.SemaphoreType.DMA((3,)),
        ],
        compiler_params=params(48),
        name="outputs",
    )(where, mine, other, table, kept)


def sketch_table(sketch_perm, rank):
    target = sketch_perm % rank
    sign = 1.0 - 2.0 * (sketch_perm // rank % 2).astype(F32)
    hit = target[:, None] == jnp.arange(rank, dtype=jnp.int32)[None, :]
    return jnp.where(hit, sign[:, None], jnp.zeros((), F32)).astype(BF16)


def swap(value):
    return lax.ppermute(value, "cols", [(0, 1), (1, 0)])


def per_device(factor, gates, gate_layout, jump_masks, jump_rates, sketch_perm, bases, basis_index):
    rows, width = factor.shape
    count = lax.axis_size("wide")
    rank = width * lax.axis_size("cols")
    where = lax.axis_index("cols").astype(jnp.int32).reshape(1)
    gated = apply_gates(gates, gate_layout, factor).reshape(2 * count, -1, width)
    moved = lax.all_to_all(gated, ("wide", "cols"), split_axis=0, concat_axis=0, tiled=True)
    moved = moved.reshape(count, 2, -1, width)
    table = sketch_table(sketch_perm, rank)
    flips = jnp.concatenate([jnp.zeros((1,), jnp.int32), jump_masks])
    coefs = jnp.concatenate([1.0 - 0.5 * jnp.sum(jump_rates, keepdims=True), jnp.sqrt(jump_rates)])
    sketch, keep, send = stack_products(where, flips, coefs, moved, table)
    part = keep + swap(send)
    part, sketch = lax.optimization_barrier((part, sketch))
    total, other = sum_wide(part, swap(sketch))
    turned = rotate_sketch(where, basis_index, sketch, other, bases)
    total, turned = lax.optimization_barrier((total, turned))
    new, weights = outputs(where, total, swap(total), table, turned)
    return new.reshape(rows, width), weights


def solution(mesh):
    return jax.shard_map(
        per_device,
        mesh=mesh,
        in_specs=(P("wide", "cols"), P(), P("wide"), P(), P(), P(), P(), P("wide", None)),
        out_specs=(P("wide", "cols"), P("wide", "cols")),
        check_vma=False,
    )
```
